128 devices in a mesh: dp: 16 (over x, z), ctx: 8 (over y, core).
Axes of the slice: x: 4, y: 4, z: 4, core: 2. Of those that a mesh axis runs over, the one named last changes fastest.
Arguments:
- patches: bfloat16 [4096, 5120], P('dp'), may hold values from -6 to 6
- vit_gain: float32 [1280], replicated, may hold values from 0.1 to 1.9
- merge_up: bfloat16 [5120, 3072], P(None, 'ctx'), may hold values from -0.078125 to 0.078125
- merge_down: bfloat16 [3072, 8192], P('ctx'), may hold values from -0.109375 to 0.109375
- dest: int32 [4096], P(('dp', 'ctx')), may hold values from 0 to 16383, as said below
- text: bfloat16 [16, 1024, 8192], P('dp', 'ctx'), may hold values from -6 to 6
- norm_gain: float32 [8192], replicated, may hold values from 0.5 to 1.5
- kv_weight: bfloat16 [8192, 1024], P(('dp', 'ctx')), may hold values from -0.0625 to 0.0625
- queries: bfloat16 [16, 1024, 4096], P('dp', 'ctx'), may hold values from -256 to 256
- out_grad: bfloat16 [16, 1024, 4096], P('dp', 'ctx'), may hold values from -6 to 6
- assign: int32 [16], replicated, may hold values from 0 to 15, each once
- docs: int32 [16, 1024], P('dp'), may hold values from 0 to 3, never falling along the last dimension, each value on 1 to 512 neighbouring positions
Outputs:
- attn_out: bfloat16 [16, 1024, 4096], P('dp', 'ctx')
- q_grad: bfloat16 [16, 1024, 4096], P('dp', 'ctx')
- hidden_grad: bfloat16 [16, 1024, 8192], P('dp', 'ctx')
- visual_grad: bfloat16 [4096, 8192], P(('dp', 'ctx'))
The draws below stay inside these ranges and needn't reach their ends.
Inputs may be any that keep to these rules, and one draw needn't show every extreme that they name: `dest`: all entries are distinct. The 32 entries held by one device name rows of 32 devices' blocks of 128 rows per device (row // 128 names the device), each such device named by exactly one entry of the holding device. Every device's block receives exactly 32 entries, which fill one run of consecutive rows, in the order of the entries' index within their holding device.
All inputs are finite; a program needn't handle non-finite values.
Results may differ from the reference program's by a relative error of at most 0.035.
Values may be sent and summed in bfloat16 or wider, within the bound.
A program may use at most 192 MiB of HBM per device.

```python
import math
import jax
import jax.numpy as jnp
import numpy as np
from jax import lax

D = 8192
VW = 1280
MH = 3072
HEADS = 32
KVH = 4
HD = 128
DOCS = 4
TOK_DEV = 128
VTOK_DEV = 32
SEQS = 16
LEN = 1024
VIS = 4096
CAP = 1
N_DP = 16
N_CTX = 8


def draw_dest(key, part):
    splits = jax.random.split(jax.random.fold_in(key, 11), 4)
    device_total = N_DP * N_CTX
    group_total = VTOK_DEV // CAP
    relabel = jax.random.permutation(splits[0], device_total)
    shuffle = jax.random.permutation(splits[1], device_total)
    offsets = jax.random.permutation(splits[2], device_total)[:group_total]
    starts = jax.random.randint(splits[3], (device_total,), 0, TOK_DEV - VTOK_DEV + 1)
    source = jnp.arange(device_total, dtype=jnp.int32)[:, None]
    token_index = jnp.arange(VTOK_DEV, dtype=jnp.int32)[None, :]
    target = relabel[(shuffle[source] + offsets[token_index // CAP]) % device_total]
    row_index = starts[target] + token_index
    return (target * TOK_DEV + row_index).reshape(VIS).astype(jnp.int32)


def draw_queries(key, part):
    base_key = jax.random.fold_in(jax.random.fold_in(key, 23), 0)
    values = jax.random.normal(base_key, (SEQS, LEN, HEADS * HD), jnp.float32)
    return jnp.clip(values, -256.0, 256.0).astype(jnp.bfloat16)


def steps_of(key, dims, cuts, smallest, largest):
    factor_of = 1.0
    for axis_at, parts in cuts:
        heights = jax.random.uniform(jax.random.fold_in(jax.random.fold_in(key, 6), axis_at), (parts,), jnp.float32, smallest / len(cuts), largest / len(cuts))
        factor_of = factor_of * jnp.repeat(jnp.exp(heights), dims[axis_at] // parts).reshape((-1,) + (1,) * (len(dims) - 1 - axis_at))
    return factor_of


def length_profile(amount, total, bound, skew):
    portions = [(1 << 20) // math.isqrt(rank ** skew) + 1 for rank in range(2, amount + 1)]
    surplus, given = total - bound - (amount - 1), [1] * (amount - 1)
    while surplus > 0:
        movable = [i for i in range(amount - 1) if given[i] < bound]
        whole, remaining = sum([portions[i] for i in movable]), surplus
        for i in movable:
            more = min(bound - given[i], max(1, remaining * portions[i] // whole), surplus)
            given[i] = given[i] + more
            surplus = surplus - more
    return np.array([bound] + given)


def ragged(rng, amount, total, bound, slope):
    if amount == 2:
        one = jax.random.randint(rng, (), max(1, total - bound), min(bound, total - 1) + 1)
        return jnp.stack([one, total - one])
    lengths = jnp.asarray(length_profile(amount, total, bound, slope), jnp.int32)
    pairs = (amount - 1) // 2
    source_of, sink = lengths[1:1 + 2 * pairs:2], lengths[2:2 + 2 * pairs:2]
    slack = jnp.minimum(source_of - 1, bound - sink)
    shifted = jax.random.randint(jax.random.fold_in(rng, 1), (pairs,), 0, 1 << 20) % (slack + 1)
    lengths = lengths.at[1:1 + 2 * pairs:2].set(source_of - shifted).at[2:2 + 2 * pairs:2].set(sink + shifted)
    return lengths[jax.random.permutation(jax.random.fold_in(rng, 2), amount)]


def normal_values(rng, shape, deviation, most, shards=(), held_as=jnp.bfloat16):
    array = jax.random.normal(rng, shape, jnp.float32) * deviation
    if len(shards) > 0:
        array = steps_of(rng, shape, shards, -0.22, 0.18) * array
    return jnp.clip(array, min=-most, max=most).astype(held_as)


def setup_inputs(seed: int = 0) -> dict:
    keys = jax.random.split(jax.random.key(seed), 13)
    patches = normal_values(keys[0], (VIS, 4 * VW), 1.0, 6.0, ((0, 16),))
    vit_gain = jnp.clip(1.0 + 0.18 * jax.random.normal(keys[1], (VW,), jnp.float32), 0.1, 1.9)
    merge_up = normal_values(keys[2], (4 * VW, MH), (4 * VW) ** -0.5, 0.078125, ((1, 8),))
    merge_down = normal_values(keys[3], (MH, D), MH ** -0.5, 0.109375, ((0, 8),))
    dest = draw_dest(jax.random.fold_in(keys[12], 71), 0)
    text = normal_values(keys[5], (SEQS, LEN, D), 1.0, 6.0, ((0, 16), (1, 8)))
    norm_gain = jnp.clip(1.0 + 0.1 * jax.random.normal(keys[6], (D,), jnp.float32), 0.5, 1.5)
    kv_weight = normal_values(keys[7], (D, 2 * KVH * HD), D ** -0.5, 0.0625, ((0, 128),))
    queries = draw_queries(jax.random.fold_in(keys[12], 71), 0)
    out_grad = normal_values(keys[9], (SEQS, LEN, HEADS * HD), 1.0, 6.0, ((0, 16), (1, 8)))
    assign = jax.random.permutation(keys[10], 2 * N_CTX).astype(jnp.int32)
    docs = jax.vmap(lambda own: jnp.searchsorted(jnp.cumsum(ragged(own, DOCS, LEN, LEN // 2, 2)), jnp.arange(LEN), side="right"))(jax.random.split(keys[11], SEQS)).reshape((SEQS, LEN)).astype(jnp.int32)
    return {"patches": patches, "vit_gain": vit_gain, "merge_up": merge_up, "merge_down": merge_down, "dest": dest, "text": text, "norm_gain": norm_gain, "kv_weight": kv_weight, "queries": queries, "out_grad": out_grad, "assign": assign, "docs": docs}


epsilon = 1e-06

def rounded(values):
    return lax.optimization_barrier(values.astype(jnp.bfloat16)).astype(jnp.float32)

def merger_norm(patches, vit_gain):
    pieces = patches.astype(jnp.float32).reshape(patches.shape[0], 4, vit_gain.shape[0])
    center = pieces - lax.optimization_barrier(jnp.mean(pieces, axis=-1, keepdims=True))
    spread = lax.optimization_barrier(jnp.mean(center * center, axis=-1, keepdims=True))
    scaled = center * lax.rsqrt(spread + epsilon) * vit_gain.astype(jnp.float32)
    return scaled.reshape(patches.shape[0], -1).astype(jnp.bfloat16)

def rms_scale(hidden32, norm_gain):
    square = lax.optimization_barrier(jnp.mean(hidden32 * hidden32, axis=-1, keepdims=True))
    return hidden32 * lax.rsqrt(square + epsilon) * norm_gain.astype(jnp.float32)

def attend_exact(query_rows, pair_rows, upstream_rows, query_pos, query_doc, key_pos, key_doc):
    row_count = query_rows.shape[0]
    key_count = pair_rows.shape[0]
    group_size = HEADS // KVH
    score_scale = HD ** (-0.5)
    query_heads = query_rows.astype(jnp.float32).reshape(row_count, KVH, group_size, HD)
    key_heads = pair_rows[:, :KVH * HD].astype(jnp.float32).reshape(key_count, KVH, HD)
    value_heads = pair_rows[:, KVH * HD:].astype(jnp.float32).reshape(key_count, KVH, HD)
    scores = jnp.einsum('qhgd,khd->hgqk', query_heads, key_heads) * score_scale
    allowed = (key_pos[None, :] <= query_pos[:, None]) & (key_doc[None, :] == query_doc[:, None])
    scores = jnp.where(allowed, scores, -jnp.inf)
    weights = jnp.exp(scores - lax.optimization_barrier(jnp.max(scores, axis=-1, keepdims=True)))
    weights = weights / lax.optimization_barrier(jnp.sum(weights, axis=-1, keepdims=True))
    light_weights = rounded(weights)
    output = jnp.einsum('hgqk,khd->qhgd', light_weights, value_heads).reshape(row_count, HEADS * HD)
    upstream = upstream_rows.astype(jnp.float32).reshape(row_count, KVH, group_size, HD)
    value_grad = jnp.einsum('hgqk,qhgd->khd', light_weights, upstream).reshape(key_count, KVH * HD)
    weight_grad = jnp.einsum('qhgd,khd->hgqk', upstream, value_heads)
    inner_sum = lax.optimization_barrier(jnp.sum(weights * weight_grad, axis=-1, keepdims=True))
    score_grad = rounded(weights * (weight_grad - inner_sum) * score_scale)
    query_grad = jnp.einsum('hgqk,khd->qhgd', score_grad, key_heads).reshape(row_count, HEADS * HD)
    key_grad = jnp.einsum('hgqk,qhgd->khd', score_grad, query_heads).reshape(key_count, KVH * HD)
    return (output.astype(jnp.bfloat16), query_grad.astype(jnp.bfloat16), key_grad, value_grad)

def reference(patches, vit_gain, merge_up, merge_down, dest, text, norm_gain, kv_weight, queries, out_grad, assign, docs):
    normed = merger_norm(patches, vit_gain)
    inner_hidden = jax.nn.gelu(jnp.dot(normed, merge_up, preferred_element_type=jnp.float32), approximate=False).astype(jnp.bfloat16)
    slice_width = MH // N_CTX
    running = jnp.zeros((VIS, D), jnp.float32)
    for group_number in range(N_CTX):
        offset = group_number * slice_width
        partial_sum = jnp.dot(inner_hidden[:, offset:offset + slice_width], merge_down[offset:offset + slice_width], preferred_element_type=jnp.float32)
        running = running + rounded(partial_sum)
    visual = running.astype(jnp.bfloat16)
    flattened = text.reshape(SEQS * LEN, D).at[dest].set(visual)
    marked = jnp.zeros((SEQS * LEN,), jnp.bool_).at[dest].set(True)
    hidden32 = flattened.astype(jnp.float32)
    normed_hidden = rms_scale(hidden32, norm_gain).astype(jnp.bfloat16)
    pairs = jnp.dot(normed_hidden, kv_weight, preferred_element_type=jnp.float32).astype(jnp.bfloat16)
    pairs = pairs.reshape(SEQS, LEN, 2 * KVH * HD)
    halves = TOK_DEV // 2
    positions = (assign[:, None] * halves + jnp.arange(halves, dtype=jnp.int32)[None, :]).reshape(LEN).astype(jnp.int32)

    def one_sequence(operands):
        query_rows, pair_rows, upstream_rows, doc_row = operands
        labels = doc_row.reshape(-1, halves)[assign].reshape(LEN)
        return attend_exact(query_rows, pair_rows, upstream_rows, positions, labels, positions, labels)
    attn_out, q_grad, key_grad, value_grad = lax.map(one_sequence, (queries, pairs, out_grad, docs))
    pair_grad = jnp.concatenate([key_grad, value_grad], axis=-1).reshape(SEQS * LEN, 2 * KVH * HD).astype(jnp.bfloat16)
    normed_grad = jnp.dot(pair_grad, kv_weight.T, preferred_element_type=jnp.float32)
    forward_value, pullback = jax.vjp(lambda values: rms_scale(values, norm_gain), hidden32)
    full_grad = pullback(normed_grad)[0]
    hidden_grad = jnp.where(marked[:, None], jnp.float32(0.0), full_grad).astype(jnp.bfloat16).reshape(SEQS, LEN, D)
    visual_grad = full_grad[dest].astype(jnp.bfloat16)
    return (attn_out, q_grad, hidden_grad, visual_grad)
```

```python
import functools
import math

import jax
import jax.numpy as jnp
from jax import lax
from jax.experimental import pallas as pl
from jax.experimental.pallas import tpu as pltpu
from jax.sharding import PartitionSpec as P

MESH = pl.DeviceIdType.MESH
BF = jnp.bfloat16
F32 = jnp.float32
HEADS = 32
KVH = 4
HD = 128
GROUP = HEADS // KVH
EPS = 1e-06
ANY = pl.BlockSpec(memory_space=pl.ANY)
VM = pl.BlockSpec(memory_space=pltpu.VMEM)


def place():
    dp, ctx = lax.axis_index("dp"), lax.axis_index("ctx")
    return {"x": dp // 4, "z": dp % 4, "y": ctx // 2, "k": ctx % 2}


def device(at):
    return (at["x"] * 4 + at["z"], at["y"] * 2 + at["k"])


def shifted(at, axis, by):
    size = 2 if axis == "k" else 4
    return dict(at, **{axis: lax.rem(at[axis] + by + size, size)})


def remote(src, dst, send, recv, to):
    return pltpu.make_async_remote_copy(
        src_ref=src, dst_ref=dst, send_sem=send, recv_sem=recv, device_id=to, device_id_type=MESH
    )


def greet(devices):
    barrier = pltpu.get_barrier_semaphore()
    for to in devices:
        pl.semaphore_signal(barrier, inc=1, device_id=to, device_id_type=MESH)
    pl.semaphore_wait(barrier, len(devices))


class Ring:
    def __init__(self, at, axis, slab, send, recv, base):
        self.at, self.axis, self.slab, self.send, self.recv, self.base = at, axis, slab, send, recv, base
        self.plus, self.minus = device(shifted(at, axis, 1)), device(shifted(at, axis, -1))
        self.sent = []

    def _coordinate(self, by):
        return shifted(self.at, self.axis, by)[self.axis]

    def _copy(self, by, half, number, to):
        ref = self.slab(self._coordinate(by), half)
        copy = remote(ref, ref, self.send.at[self.base + number], self.recv.at[self.base + number], to)
        copy.start()
        self.sent.append(copy)

    def start(self):
        self._copy(0, 0, 0, self.plus)
        self._copy(0, 1, 1, self.minus)
        self._copy(0, 1, 2, self.plus)
        self._copy(0, 0, 3, self.minus)

    ARRIVALS = ((-1, 0), (1, 1), (-1, 1), (1, 0), (2, 0), (2, 1))

    def arrived(self, number):
        by, half = self.ARRIVALS[number]
        ref = self.slab(self._coordinate(by), half)
        remote(ref, ref, self.send.at[self.base + number], self.recv.at[self.base + number], self.plus).wait_recv()
        return ref

    def relay(self):
        first, second = self.arrived(0), self.arrived(1)
        self._copy(-1, 0, 4, self.plus)
        self._copy(1, 1, 5, self.minus)
        return first, second

    def finish(self):
        for copy in self.sent:
            copy.wait_send()


class RingSum:
    def __init__(self, at, sums, far, plain, through, chunks, send, recv):
        self.at, self.sums, self.far, self.plain, self.through = at, sums, far, plain, through
        self.chunks, self.send, self.recv = chunks, send, recv
        self.width = sums.shape[2] // chunks
        self.sent = []

    def _block(self, by, chunk):
        y = shifted(self.at, "y", by)["y"]
        return self.sums.at[y, :, pl.ds(chunk * self.width, self.width)]

    def _way(self, chunk):
        return 1 if chunk < self.chunks // 2 else -1

    def _copy(self, src, dst, number, by):
        copy = remote(src, dst, self.send.at[number], self.recv.at[number], device(shifted(self.at, "y", by)))
        copy.start()
        self.sent.append(copy)

    def _wait(self, dst, number):
        remote(dst, dst, self.send.at[number], self.recv.at[number], device(shifted(self.at, "y", 1))).wait_recv()

    def start(self, chunk):
        way = self._way(chunk)
        self._copy(self._block(2, chunk), self.far.at[chunk], chunk * 3, way)
        self._copy(self._block(-way, chunk), self.plain.at[chunk], chunk * 3 + 1, -way)

    def relay(self, chunk):
        way = self._way(chunk)
        self._wait(self.far.at[chunk], chunk * 3)
        block = self._block(way, chunk)
        block[...] = (block[...].astype(F32) + self.far[chunk].astype(F32)).astype(BF)
        self._copy(block, self.through.at[chunk], chunk * 3 + 2, way)

    def total(self, chunk):
        self._wait(self.plain.at[chunk], chunk * 3 + 1)
        self._wait(self.through.at[chunk], chunk * 3 + 2)
        own = self._block(0, chunk)[...].astype(F32)
        return own + self.plain[chunk].astype(F32) + self.through[chunk].astype(F32)

    def finish(self):
        for copy in self.sent:
            copy.wait_send()


PARTS = ((0, 384, "yzx"), (384, 384, "yxz"), (768, 256, "xzy"))
ORDER = (0, 2, 1, 3)


def first_kernel(
    patches_hbm, vit_gain, up_hbm, down_hbm, text_hbm, gain, kv_hbm, slot_of, row_of,
    weight_out, outgoing, text_pairs, visual_pairs, visual_out, scales,
    weight, patches, up, down, text, normed, hidden, partial, from_partner, sums, far, plain, through, acc, inner,
    load, send, recv, forward_send, forward_recv, pair_send, pair_recv, sum_send, sum_recv,
):
    at = place()
    k, y = at["k"], at["y"]
    chip = (at["x"] * 4 + at["z"]) * 4 + y
    own = pltpu.make_async_copy(kv_hbm, weight.at[chip, k], load.at[0])
    own.start()
    loads = []
    for number, (src, dst) in enumerate(((patches_hbm, patches), (up_hbm, up), (down_hbm, down), (text_hbm, text))):
        copy = pltpu.make_async_copy(src, dst, load.at[number + 1])
        copy.start()
        loads.append(copy)
    partner = device(shifted(at, "k", 1))
    greet([device(shifted(at, axis, by)) for axis in "xyz" for by in (1, -1)] + [partner])
    own.wait()

    def slab_of(axes_done, axis, first, count):
        def slab(coordinate, half):
            cut = {name: (pl.ds(0, 4) if name in axes_done else pl.ds(at[name], 1)) for name in "xyz"}
            cut[axis] = pl.ds(coordinate, 1)
            view = weight.reshape(4, 4, 4, 2, 64, 1024) if False else weight6
            return view.at[cut["x"], cut["z"], cut["y"], k, pl.ds(32 * half, 32), pl.ds(first, count)]

        return slab

    weight6 = weight.reshape(4, 4, 4, 2, 64, 1024)
    rings = [
        [
            Ring(at, order[phase], slab_of(order[:phase], order[phase], first, count), send, recv, (part * 3 + phase) * 6)
            for phase in range(3)
        ]
        for part, (first, count, order) in enumerate(PARTS)
    ]
    forwards = []

    def forward(ref, number):
        copy = remote(ref, ref, forward_send.at[number], forward_recv.at[number], partner)
        copy.start()
        forwards.append(copy)

    for part in rings:
        part[0].start()

    loads[0].wait()
    vg = vit_gain[...]

    def norm_rows(step, carry):
        rows = pl.ds(pl.multiple_of(step * 16, 16), 16)
        for piece in range(4):
            columns = pl.ds(piece * 1280, 1280)
            value = patches[rows, columns].astype(F32)
            center = value - jnp.mean(value, axis=-1, keepdims=True)
            spread = jnp.mean(center * center, axis=-1, keepdims=True)
            patches[rows, columns] = (center * lax.rsqrt(spread + EPS) * vg).astype(BF)
        return carry

    lax.fori_loop(0, 16, norm_rows, 0)
    for part in rings:
        part[0].relay()

    loads[1].wait()
    inner[...] = jnp.zeros_like(inner)

    def up_step(step, carry):
        columns = pl.ds(pl.multiple_of(step * 1024, 1024), 1024)
        inner[...] += jnp.dot(patches[:, columns], up[columns, :], preferred_element_type=F32)
        return carry

    lax.fori_loop(0, 5, up_step, 0)
    for part in rings:
        for number in (2, 3, 4, 5):
            part[0].arrived(number)
        part[1].start()
    value = inner[...]
    hidden[...] = (0.5 * value * (1.0 + lax.erf(value * (1.0 / math.sqrt(2.0))))).astype(BF)
    loads[2].wait()

    width = 2048
    swaps = {}
    for chunk in ORDER:
        def down_step(step, carry, chunk=chunk):
            columns = pl.ds(pl.multiple_of(chunk * width + step * 512, 512), 512)
            product = jnp.dot(hidden[...], down[:, columns], preferred_element_type=F32)
            partial[:, :, :, columns] = product.astype(BF).reshape(4, 2, 32, 512)
            return carry

        lax.fori_loop(0, 4, down_step, 0)
        columns = pl.ds(chunk * width, width)
        swaps[chunk] = remote(
            partial.at[:, 1 - k, :, columns], from_partner.at[:, :, columns], pair_send.at[chunk], pair_recv.at[chunk], partner
        )
        swaps[chunk].start()
        if chunk == 2:
            for part in rings:
                part[1].relay()
    ring_sum = RingSum(at, sums, far, plain, through, 4, sum_send, sum_recv)
    for chunk in ORDER:
        swaps[chunk].wait_recv()
        columns = pl.ds(chunk * width, width)
        for block in range(4):
            mine = partial[block, pl.ds(k, 1), :, columns].reshape(32, width)
            sums[block, :, columns] = (mine.astype(F32) + from_partner[block, :, columns].astype(F32)).astype(BF)
        ring_sum.start(chunk)
    for number, part in enumerate(rings):
        for arrival in (2, 3, 4, 5):
            part[1].arrived(arrival)
        part[2].start()
        order = PARTS[number][2]
        cut = {name: (pl.ds(at[name], 1) if name == order[2] else pl.ds(0, 4)) for name in "xyz"}
        forward(weight6.at[cut["x"], cut["z"], cut["y"], k, :, pl.ds(PARTS[number][0], PARTS[number][1])], number * 7)

    loads[3].wait()

    def text_rows(step, carry):
        rows = pl.ds(pl.multiple_of(step * 16, 16), 16)
        value = text[rows, :].astype(F32)
        scale = lax.rsqrt(jnp.mean(value * value, axis=-1, keepdims=True) + EPS)
        normed[rows, :] = (value * scale * gain[...]).astype(BF)
        scales[rows, :] = jnp.broadcast_to(scale, (16, 128))
        return carry

    lax.fori_loop(0, 8, text_rows, 0)
    for chunk in ORDER:
        ring_sum.relay(chunk)
    for number, part in enumerate(rings):
        first, second = part[2].relay()
        forward(first, number * 7 + 1)
        forward(second, number * 7 + 2)
    for number, part in enumerate(rings):
        for arrival in (2, 3):
            forward(part[2].arrived(arrival), number * 7 + 1 + arrival)
    for chunk in ORDER:
        visual_out[:, pl.ds(chunk * width, width)] = ring_sum.total(chunk).astype(BF)
    for step in range(2):
        rows = pl.ds(step * 16, 16)
        value = visual_out[rows, :].astype(F32)
        scale = lax.rsqrt(jnp.mean(value * value, axis=-1, keepdims=True) + EPS)
        normed[pl.ds(128 + step * 16, 16), :] = (value * scale * gain[...]).astype(BF)
        scales[pl.ds(128 + step * 16, 16), :] = jnp.broadcast_to(scale, (16, 128))
    for number, part in enumerate(rings):
        for arrival in (4, 5):
            forward(part[2].arrived(arrival), number * 7 + 1 + arrival)
    for copy in forwards:
        copy.wait_recv()
    out = pltpu.make_async_copy(weight, weight_out, load.at[5])
    out.start()
    acc[...] = jnp.zeros_like(acc)

    def project(step, carry):
        columns = pl.ds(pl.multiple_of(step * 512, 512), 512)
        block = weight[pl.ds(step * 4, 4)].reshape(512, 1024)
        acc[...] += jnp.dot(normed[:, columns], block, preferred_element_type=F32)
        return carry

    lax.fori_loop(0, 16, project, 0)
    text_pairs[...] = acc[pl.ds(0, 128), :].astype(BF)
    mine = acc[pl.ds(128, 32), :].astype(BF)
    visual_pairs[...] = mine
    picking = (lax.broadcasted_iota(jnp.int32, (128, 32), 0) == slot_of[...]).astype(F32).astype(BF)
    outgoing[:, :, pl.ds(0, 1024)] = jnp.dot(picking, mine, preferred_element_type=F32).astype(BF).reshape(8, 16, 1024)
    outgoing[:, :, pl.ds(1024, 128)] = jnp.dot(picking, row_of[...], preferred_element_type=F32).astype(BF).reshape(8, 16, 128)
    for part in rings:
        for ring in part:
            ring.finish()
    for copy in forwards:
        copy.wait_send()
    for chunk in ORDER:
        swaps[chunk].wait_send()
    ring_sum.finish()
    out.wait()


def first_call(patches, vit_gain, up, down, text, gain, kv, slot_of, row_of):
    shape = jax.ShapeDtypeStruct
    dma = pltpu.SemaphoreType.DMA
    return pl.pallas_call(
        first_kernel,
        out_shape=(
            shape((64, 2, 64, 1024), BF), shape((8, 16, 1152), BF), shape((128, 1024), BF), shape((32, 1024), BF),
            shape((32, 8192), BF), shape((160, 128), F32),
        ),
        in_specs=[ANY, VM, ANY, ANY, ANY, VM, ANY, VM, VM],
        out_specs=(ANY, VM, VM, VM, VM, VM),
        scratch_shapes=[
            pltpu.VMEM((64, 2, 64, 1024), BF), pltpu.VMEM((256, 5120), BF), pltpu.VMEM((5120, 384), BF),
            pltpu.VMEM((384, 8192), BF), pltpu.VMEM((128, 8192), BF), pltpu.VMEM((160, 8192), BF), pltpu.VMEM((256, 384), BF),
            pltpu.VMEM((4, 2, 32, 8192), BF), pltpu.VMEM((4, 32, 8192), BF), pltpu.VMEM((4, 32, 8192), BF),
            pltpu.VMEM((4, 32, 2048), BF), pltpu.VMEM((4, 32, 2048), BF), pltpu.VMEM((4, 32, 2048), BF),
            pltpu.VMEM((160, 1024), F32), pltpu.VMEM((256, 384), F32),
            dma((6,)), dma((54,)), dma((54,)), dma((21,)), dma((21,)), dma((4,)), dma((4,)), dma((12,)), dma((12,)),
        ],
        compiler_params=pltpu.CompilerParams(collective_id=1, has_side_effects=True, vmem_limit_bytes=62 * 2**20),
        name="merge_and_project",
    )(patches, vit_gain, up, down, text, gain, kv, slot_of, row_of)


def exchange_kernel(
    outgoing, text_pairs, pairs, placing, marked,
    landed, turned, arrived, load, ctx_send, ctx_recv, dp_send, dp_recv, send, recv, forward_send, forward_recv,
):
    at = place()
    dp, ctx = lax.axis_index("dp"), lax.axis_index("ctx")
    k, y = at["k"], at["y"]
    greet([(dp, lax.rem(ctx + by, 8)) for by in range(1, 8)] + [(lax.rem(dp + by, 16), ctx) for by in range(1, 16)])
    own = pltpu.make_async_copy(outgoing.at[ctx], landed.at[ctx], load.at[0])
    own.start()
    copies = []
    for by in range(1, 8):
        to = lax.rem(ctx + by, 8)
        copy = remote(outgoing.at[to], landed.at[ctx], ctx_send.at[by - 1], ctx_recv.at[by - 1], (dp, to))
        copy.start()
        copies.append(copy)
    own.wait()
    for by in range(1, 8):
        source = lax.rem(ctx - by + 8, 8)
        remote(landed.at[source], landed.at[source], ctx_send.at[by - 1], ctx_recv.at[by - 1], (dp, source)).wait_recv()
    row = lax.broadcasted_iota(jnp.int32, (128, 128), 0)
    turn = (lax.broadcasted_iota(jnp.int32, (128, 128), 1) == (row % 8) * 16 + row // 8).astype(F32).astype(BF)
    turned[...] = jnp.dot(turn, landed[...].reshape(128, 1152), preferred_element_type=F32).reshape(16, 8, 1152).astype(BF)
    own = pltpu.make_async_copy(turned.at[dp], arrived.at[dp], load.at[1])
    own.start()
    for by in range(1, 16):
        to = lax.rem(dp + by, 16)
        copy = remote(turned.at[to], arrived.at[dp], dp_send.at[by - 1], dp_recv.at[by - 1], (to, ctx))
        copy.start()
        copies.append(copy)
    own.wait()
    for by in range(1, 16):
        source = lax.rem(dp - by + 16, 16)
        remote(arrived.at[source], arrived.at[source], dp_send.at[by - 1], dp_recv.at[by - 1], (source, ctx)).wait_recv()
    rows = arrived[:, :, pl.ds(1024, 128)].astype(F32).reshape(128, 128)
    lane = lax.broadcasted_iota(jnp.int32, (128, 128), 1).astype(F32) + 1.0
    places = (rows == lane).astype(F32).astype(BF)
    placing[...] = places
    contract = (((0,), (0,)), ((), ()))
    values = arrived[:, :, pl.ds(0, 1024)].astype(F32).reshape(128, 1024).astype(BF)
    placed = lax.dot_general(places, values, contract, preferred_element_type=F32)
    mark = lax.dot_general(places, jnp.ones((128, 128), BF), contract, preferred_element_type=F32)
    marked[...] = mark
    pairs[y, k] = jnp.where(mark[:, :1] > 0.5, placed, text_pairs[...].astype(F32)).astype(BF)

    partner = device(shifted(at, "k", 1))
    ring = Ring(at, "y", lambda coordinate, half: pairs.at[coordinate, k, pl.ds(64 * half, 64)], send, recv, 0)
    forwards = []

    def forward(ref, number):
        copy = remote(ref, ref, forward_send.at[number], forward_recv.at[number], partner)
        copy.start()
        forwards.append(copy)

    ring.start()
    forward(pairs.at[y, k], 0)
    first, second = ring.relay()
    forward(first, 1)
    forward(second, 2)
    for number in (2, 3, 4, 5):
        forward(ring.arrived(number), number + 1)
    for copy in forwards:
        copy.wait()
    for copy in copies:
        copy.wait_send()
    ring.finish()


def exchange_call(outgoing, text_pairs):
    shape = jax.ShapeDtypeStruct
    dma = pltpu.SemaphoreType.DMA
    return pl.pallas_call(
        exchange_kernel,
        out_shape=(shape((4, 2, 128, 1024), BF), shape((128, 128), BF), shape((128, 128), F32)),
        in_specs=[VM, VM],
        out_specs=(VM, VM, VM),
        scratch_shapes=[
            pltpu.VMEM((8, 16, 1152), BF), pltpu.VMEM((16, 8, 1152), BF), pltpu.VMEM((16, 8, 1152), BF),
            dma((2,)), dma((7,)), dma((7,)), dma((15,)), dma((15,)), dma((6,)), dma((6,)), dma((7,)), dma((7,)),
        ],
        compiler_params=pltpu.CompilerParams(collective_id=2, has_side_effects=True),
        name="exchange_pairs",
    )(outgoing, text_pairs)


WINDOW = 640


def attend_kernel(assign, own, pairs_hbm, docs, queries, upstream, attn_out, q_grad, pair_grads, held, turned, load):
    head = pl.program_id(0)

    @pl.when(head == 0)
    def _():
        for block in range(16):
            pltpu.make_async_copy(pairs_hbm.at[block], held.at[assign[block]], load.at[block]).start()
        for block in range(16):
            pltpu.make_async_copy(pairs_hbm.at[block], held.at[assign[block]], load.at[block]).wait()

    labels = docs[...]
    starts = [jnp.sum((labels < d).astype(F32)).astype(jnp.int32) for d in (1, 2, 3)]
    key_columns = pl.ds(pl.multiple_of(head * HD, HD), HD)
    value_columns = pl.ds(pl.multiple_of(KVH * HD + head * HD, HD), HD)
    turned[...] = jnp.zeros_like(turned)
    score_scale = HD**-0.5
    outer = (((0,), (0,)), ((), ()))
    inner = (((1,), (1,)), ((), ()))
    for half in range(2):
        position = assign[own[0] * 2 + half]
        low = jnp.maximum(position // 2 - 4, 0)
        rows = pl.ds(half * 64, 64)
        query = jnp.concatenate([queries[rows, g * HD : (g + 1) * HD] for g in range(GROUP)], axis=0)
        grad = jnp.concatenate([upstream[rows, g * HD : (g + 1) * HD] for g in range(GROUP)], axis=0)
        blocks = pl.ds(low * 2, WINDOW // 64)
        keys = held[blocks, :, key_columns].reshape(WINDOW, HD)
        values = held[blocks, :, value_columns].reshape(WINDOW, HD)
        query_at = position * 64 + lax.broadcasted_iota(jnp.int32, (64, WINDOW), 0)
        key_at = low * 128 + lax.broadcasted_iota(jnp.int32, (64, WINDOW), 1)
        begin = jnp.zeros((64, WINDOW), jnp.int32)
        for start in starts:
            begin = jnp.where(query_at >= start, start, begin)
        allowed = (key_at <= query_at) & (key_at >= begin)
        scores = lax.dot_general(query, keys, inner, preferred_element_type=F32).reshape(GROUP, 64, WINDOW)
        scores = jnp.where(allowed[None], scores * (score_scale * math.log2(math.e)), -1e30)
        weights = jnp.exp2(scores - jnp.max(scores, axis=-1, keepdims=True))
        weights = weights * (1.0 / jnp.sum(weights, axis=-1, keepdims=True))
        weights = weights.reshape(GROUP * 64, WINDOW)
        light = weights.astype(BF)
        output = jnp.dot(light, values, preferred_element_type=F32)
        weight_grad = lax.dot_general(grad, values, inner, preferred_element_type=F32)
        inner_sum = jnp.sum(weights * weight_grad, axis=-1, keepdims=True)
        score_grad = (weights * (weight_grad - inner_sum)).astype(BF)
        query_grad = jnp.dot(score_grad, keys, preferred_element_type=F32) * score_scale
        window = pl.ds(pl.multiple_of(low * 128, 128), WINDOW)
        turned[0, :, window] += lax.dot_general(query, score_grad, outer, preferred_element_type=F32)
        turned[1, :, window] += lax.dot_general(grad, light, outer, preferred_element_type=F32)
        for g in range(GROUP):
            attn_out[rows, g * HD : (g + 1) * HD] = output[g * 64 : (g + 1) * 64].astype(BF)
            q_grad[rows, g * HD : (g + 1) * HD] = query_grad[g * 64 : (g + 1) * 64].astype(BF)
    upright = (turned[0] * score_scale).T.reshape(16, 64, HD).astype(BF)
    straight = turned[1].T.reshape(16, 64, HD).astype(BF)
    held[:, :, key_columns] = upright
    held[:, :, value_columns] = straight
    for block in range(16):
        pair_grads[block, :, key_columns] = held[assign[block], :, key_columns]
        pair_grads[block, :, value_columns] = held[assign[block], :, value_columns]


def attend_call(assign, own, pairs, docs, queries, upstream):
    shape = jax.ShapeDtypeStruct
    by_head = pl.BlockSpec((128, GROUP * HD), lambda head, *_: (0, head))
    return pl.pallas_call(
        attend_kernel,
        out_shape=(shape((128, 4096), BF), shape((128, 4096), BF), shape((16, 64, 1024), BF)),
        grid_spec=pltpu.PrefetchScalarGridSpec(
            num_scalar_prefetch=2,
            grid=(KVH,),
            in_specs=[ANY, pl.BlockSpec((1, 1024), lambda head, *_: (0, 0)), by_head, by_head],
            out_specs=(by_head, by_head, pl.BlockSpec((16, 64, 1024), lambda head, *_: (0, 0, 0))),
            scratch_shapes=[pltpu.VMEM((16, 64, 1024), BF), pltpu.VMEM((2, HD, 1024), F32), pltpu.SemaphoreType.DMA((16,))],
        ),
        compiler_params=pltpu.CompilerParams(vmem_limit_bytes=56 * 2**20),
        name="attend",
    )(assign, own, pairs, docs, queries, upstream)


def return_kernel(
    grads, placing, slot_of, own_grad, visual_grad,
    from_partner, sums, far, plain, through, leaving, landed, turned, arrived,
    load, pair_send, pair_recv, sum_send, sum_recv, dp_send, dp_recv, ctx_send, ctx_recv,
):
    at = place()
    dp, ctx = lax.axis_index("dp"), lax.axis_index("ctx")
    k, y = at["k"], at["y"]
    greet([(dp, lax.rem(ctx + by, 8)) for by in range(1, 8)] + [(lax.rem(dp + by, 16), ctx) for by in range(1, 16)])
    partner = device(shifted(at, "k", 1))
    width = 256
    swaps = {}
    for chunk in ORDER:
        columns = pl.ds(chunk * width, width)
        swaps[chunk] = remote(
            grads.at[:, 1 - k, :, columns], from_partner.at[:, :, columns], pair_send.at[chunk], pair_recv.at[chunk], partner
        )
        swaps[chunk].start()
    ring_sum = RingSum(at, sums, far, plain, through, 4, sum_send, sum_recv)
    for chunk in ORDER:
        swaps[chunk].wait_recv()
        columns = pl.ds(chunk * width, width)
        for block in range(4):
            mine = grads[block, pl.ds(k, 1), :, columns].reshape(128, width)
            sums[block, :, columns] = (mine.astype(F32) + from_partner[block, :, columns].astype(F32)).astype(BF)
        ring_sum.start(chunk)
    for chunk in ORDER:
        ring_sum.relay(chunk)
    for chunk in ORDER:
        own_grad[:, pl.ds(chunk * width, width)] = ring_sum.total(chunk).astype(BF)
    leaving[...] = jnp.dot(placing[...], own_grad[...], preferred_element_type=F32).reshape(16, 8, 1024).astype(BF)
    own = pltpu.make_async_copy(leaving.at[dp], landed.at[dp], load.at[0])
    own.start()
    copies = []
    for by in range(1, 16):
        to = lax.rem(dp + by, 16)
        copy = remote(leaving.at[to], landed.at[dp], dp_send.at[by - 1], dp_recv.at[by - 1], (to, ctx))
        copy.start()
        copies.append(copy)
    own.wait()
    for by in range(1, 16):
        source = lax.rem(dp - by + 16, 16)
        remote(landed.at[source], landed.at[source], dp_send.at[by - 1], dp_recv.at[by - 1], (source, ctx)).wait_recv()
    row = lax.broadcasted_iota(jnp.int32, (128, 128), 0)
    turn = (lax.broadcasted_iota(jnp.int32, (128, 128), 1) == (row % 16) * 8 + row // 16).astype(F32).astype(BF)
    came = landed[...].astype(F32).reshape(128, 1024).astype(BF)
    turned[...] = jnp.dot(turn, came, preferred_element_type=F32).astype(BF).reshape(8, 16, 1024)
    own = pltpu.make_async_copy(turned.at[ctx], arrived.at[ctx], load.at[1])
    own.start()
    for by in range(1, 8):
        to = lax.rem(ctx + by, 8)
        copy = remote(turned.at[to], arrived.at[ctx], ctx_send.at[by - 1], ctx_recv.at[by - 1], (dp, to))
        copy.start()
        copies.append(copy)
    own.wait()
    for by in range(1, 8):
        source = lax.rem(ctx - by + 8, 8)
        remote(arrived.at[source], arrived.at[source], ctx_send.at[by - 1], ctx_recv.at[by - 1], (dp, source)).wait_recv()
    picking = (slot_of[...] == lax.broadcasted_iota(jnp.int32, (32, 128), 1)).astype(F32).astype(BF)
    visual_grad[...] = jnp.dot(picking, arrived[...].reshape(128, 1024), preferred_element_type=F32).astype(BF)
    for copy in copies:
        copy.wait_send()
    for chunk in ORDER:
        swaps[chunk].wait_send()
    ring_sum.finish()


def return_call(grads, placing, slot_of):
    shape = jax.ShapeDtypeStruct
    dma = pltpu.SemaphoreType.DMA
    return pl.pallas_call(
        return_kernel,
        out_shape=(shape((128, 1024), BF), shape((32, 1024), BF)),
        in_specs=[VM, VM, VM],
        out_specs=(VM, VM),
        scratch_shapes=[
            pltpu.VMEM((4, 128, 1024), BF), pltpu.VMEM((4, 128, 1024), BF),
            pltpu.VMEM((4, 128, 256), BF), pltpu.VMEM((4, 128, 256), BF), pltpu.VMEM((4, 128, 256), BF),
            pltpu.VMEM((16, 8, 1024), BF), pltpu.VMEM((16, 8, 1024), BF), pltpu.VMEM((8, 16, 1024), BF), pltpu.VMEM((8, 16, 1024), BF),
            dma((2,)), dma((4,)), dma((4,)), dma((12,)), dma((12,)), dma((15,)), dma((15,)), dma((7,)), dma((7,)),
        ],
        compiler_params=pltpu.CompilerParams(collective_id=3, has_side_effects=True),
        name="return_grads",
    )(grads, placing, slot_of)


def final_kernel(
    own_grad, visual_pair_grad, text_pairs, visual_pairs, weight, text, visual, gain, scales, marked, hidden_grad, visual_grad
):
    contract = (((1,), (1,)), ((), ()))
    block = weight[...]
    gains = gain[...]

    def through(grad, pair, value, scale):
        mean = jnp.sum(grad.astype(F32) * pair.astype(F32), axis=-1, keepdims=True) * (1.0 / 8192.0)
        normed_grad = lax.dot_general(grad, block, contract, preferred_element_type=F32)
        return scale * (gains * normed_grad) - value.astype(F32) * (scale * scale * mean)

    full = through(own_grad[...], text_pairs[...], text[...], scales[0:128, 0:1])
    hidden_grad[...] = jnp.where(marked[:, 0:1] > 0.5, 0.0, full).astype(BF)
    visual_grad[...] = through(visual_pair_grad[...], visual_pairs[...], visual[...], scales[128:160, 0:1]).astype(BF)


def final_call(own_grad, visual_pair_grad, text_pairs, visual_pairs, weight, text, visual, gain, scales, marked):
    shape = jax.ShapeDtypeStruct
    tile = 1024

    def whole(*dims):
        return pl.BlockSpec(dims, lambda i: (0,) * len(dims))

    return pl.pallas_call(
        final_kernel,
        out_shape=(shape((128, 8192), BF), shape((32, 8192), BF)),
        grid=(8192 // tile,),
        in_specs=[
            whole(128, 1024), whole(32, 1024), whole(128, 1024), whole(32, 1024),
            pl.BlockSpec((tile, 1024), lambda i: (i, 0)), pl.BlockSpec((128, tile), lambda i: (0, i)),
            pl.BlockSpec((32, tile), lambda i: (0, i)), pl.BlockSpec((1, tile), lambda i: (0, i)),
            whole(160, 128), whole(128, 128),
        ],
        out_specs=(pl.BlockSpec((128, tile), lambda i: (0, i)), pl.BlockSpec((32, tile), lambda i: (0, i))),
        compiler_params=pltpu.CompilerParams(vmem_limit_bytes=48 * 2**20),
        name="through_norm",
    )(own_grad, visual_pair_grad, text_pairs, visual_pairs, weight, text, visual, gain, scales, marked)


def local(patches, vit_gain, merge_up, merge_down, dest, text, norm_gain, kv_weight, queries, out_grad, assign, docs):
    target = dest // 128
    slot = (target % 8) * 16 + target // 8
    row_of = jnp.broadcast_to((dest % 128 + 1).astype(BF)[:, None], (32, 128))
    gain = norm_gain.reshape(1, 8192)
    weight, outgoing, text_pairs, visual_pairs, visual, scales = first_call(
        patches, vit_gain.reshape(1, 1280), merge_up, merge_down, text[0], gain, kv_weight, slot.reshape(1, 32), row_of
    )
    pairs, placing, marked = exchange_call(outgoing, text_pairs)
    own = lax.axis_index("ctx").astype(jnp.int32).reshape(1)
    attention, query_grad, pair_grads = attend_call(assign, own, pairs.reshape(16, 64, 1024), docs, queries[0], out_grad[0])
    own_grad, visual_pair_grad = return_call(
        pair_grads.reshape(4, 2, 128, 1024), placing, jnp.broadcast_to(slot[:, None], (32, 128))
    )
    hidden_grad, visual_grad = final_call(
        own_grad, visual_pair_grad, text_pairs, visual_pairs, weight.reshape(8192, 1024), text[0], visual, gain, scales, marked
    )
    return attention[None], query_grad[None], hidden_grad[None], visual_grad


def solution(mesh):
    placed = (
        P("dp", None),
        P(),
        P(None, "ctx"),
        P("ctx", None),
        P(("dp", "ctx")),
        P("dp", "ctx", None),
        P(),
        P(("dp", "ctx"), None),
        P("dp", "ctx", None),
        P("dp", "ctx", None),
        P(),
        P("dp", None),
    )
    return jax.shard_map(
        local,
        mesh=mesh,
        in_specs=placed,
        out_specs=(P("dp", "ctx", None), P("dp", "ctx", None), P("dp", "ctx", None), P(("dp", "ctx"), None)),
        check_vma=False,
    )
```

```python
import functools
import math

import jax
import jax.numpy as jnp
from jax import lax
from jax.experimental import pallas as pl
from jax.experimental.pallas import tpu as pltpu
from jax.sharding import PartitionSpec as P

MESH = pl.DeviceIdType.MESH
BF = jnp.bfloat16
F32 = jnp.float32
HEADS = 32
KVH = 4
HD = 128
GROUP = HEADS // KVH
EPS = 1e-06
ANY = pl.BlockSpec(memory_space=pl.ANY)
VM = pl.BlockSpec(memory_space=pltpu.VMEM)


def place():
    dp, ctx = lax.axis_index("dp"), lax.axis_index("ctx")
    return {"x": dp // 4, "z": dp % 4, "y": ctx // 2, "k": ctx % 2}


def device(at):
    return (at["x"] * 4 + at["z"], at["y"] * 2 + at["k"])


def shifted(at, axis, by):
    size = 2 if axis == "k" else 4
    return dict(at, **{axis: lax.rem(at[axis] + by + size, size)})


def remote(src, dst, send, recv, to):
    return pltpu.make_async_remote_copy(
        src_ref=src, dst_ref=dst, send_sem=send, recv_sem=recv, device_id=to, device_id_type=MESH
    )


def greet(devices):
    barrier = pltpu.get_barrier_semaphore()
    for to in devices:
        pl.semaphore_signal(barrier, inc=1, device_id=to, device_id_type=MESH)
    pl.semaphore_wait(barrier, len(devices))


def upright(row):
    same = lax.broadcasted_iota(jnp.int32, (32, 32), 0) == lax.broadcasted_iota(jnp.int32, (32, 32), 1)
    return jnp.sum(jnp.where(same, jnp.broadcast_to(row, (32, 32)), 0).astype(F32), axis=1, keepdims=True)


class Ring:
    def __init__(self, at, axis, slab, send, recv, base):
        self.at, self.axis, self.slab, self.send, self.recv, self.base = at, axis, slab, send, recv, base
        self.plus, self.minus = device(shifted(at, axis, 1)), device(shifted(at, axis, -1))
        self.sent = []

    def _coordinate(self, by):
        return shifted(self.at, self.axis, by)[self.axis]

    def _copy(self, by, half, number, to):
        ref = self.slab(self._coordinate(by), half)
        copy = remote(ref, ref, self.send.at[self.base + number], self.recv.at[self.base + number], to)
        copy.start()
        self.sent.append(copy)

    def start(self):
        self._copy(0, 0, 0, self.plus)
        self._copy(0, 1, 1, self.minus)
        self._copy(0, 1, 2, self.plus)
        self._copy(0, 0, 3, self.minus)

    ARRIVALS = ((-1, 0), (1, 1), (-1, 1), (1, 0), (2, 0), (2, 1))

    def arrived(self, number):
        by, half = self.ARRIVALS[number]
        ref = self.slab(self._coordinate(by), half)
        remote(ref, ref, self.send.at[self.base + number], self.recv.at[self.base + number], self.plus).wait_recv()
        return ref

    def relay(self):
        first, second = self.arrived(0), self.arrived(1)
        self._copy(-1, 0, 4, self.plus)
        self._copy(1, 1, 5, self.minus)
        return first, second

    def finish(self):
        for copy in self.sent:
            copy.wait_send()


class RingSum:
    def __init__(self, at, sums, far, plain, through, chunks, send, recv):
        self.at, self.sums, self.far, self.plain, self.through = at, sums, far, plain, through
        self.chunks, self.send, self.recv = chunks, send, recv
        self.width = sums.shape[2] // chunks
        self.sent = []

    def _block(self, by, chunk):
        y = shifted(self.at, "y", by)["y"]
        return self.sums.at[y, :, pl.ds(chunk * self.width, self.width)]

    def _way(self, chunk):
        return 1 if chunk < self.chunks // 2 else -1

    def _copy(self, src, dst, number, by):
        copy = remote(src, dst, self.send.at[number], self.recv.at[number], device(shifted(self.at, "y", by)))
        copy.start()
        self.sent.append(copy)

    def _wait(self, dst, number):
        remote(dst, dst, self.send.at[number], self.recv.at[number], device(shifted(self.at, "y", 1))).wait_recv()

    def start(self, chunk):
        way = self._way(chunk)
        self._copy(self._block(2, chunk), self.far.at[chunk], chunk * 3, way)
        self._copy(self._block(-way, chunk), self.plain.at[chunk], chunk * 3 + 1, -way)

    def relay(self, chunk):
        way = self._way(chunk)
        self._wait(self.far.at[chunk], chunk * 3)
        block = self._block(way, chunk)
        block[...] = (block[...].astype(F32) + self.far[chunk].astype(F32)).astype(BF)
        self._copy(block, self.through.at[chunk], chunk * 3 + 2, way)

    def total(self, chunk):
        self._wait(self.plain.at[chunk], chunk * 3 + 1)
        self._wait(self.through.at[chunk], chunk * 3 + 2)
        own = self._block(0, chunk)[...].astype(F32)
        return own + self.plain[chunk].astype(F32) + self.through[chunk].astype(F32)

    def finish(self):
        for copy in self.sent:
            copy.wait_send()


PARTS = ((0, 384, "yzx"), (384, 384, "xyz"), (768, 256, "zxy"))
ORDER = (0, 2, 1, 3)


def first_kernel(
    patches_hbm, vit_gain, up_hbm, down_hbm, text_hbm, gain, kv_hbm, dest,
    weight_out, outgoing, text_pairs, visual_pairs, visual_out, scales,
    weight, patches, up, down, text, normed, hidden, partial, from_partner, sums, far, plain, through, acc, inner,
    load, send, recv, forward_send, forward_recv, pair_send, pair_recv, sum_send, sum_recv, store,
):
    at = place()
    k, y = at["k"], at["y"]
    chip = (at["x"] * 4 + at["z"]) * 4 + y
    own = pltpu.make_async_copy(kv_hbm, weight.at[chip, k], load.at[0])
    own.start()
    loads = []
    for number, (src, dst) in enumerate(((patches_hbm, patches), (up_hbm, up), (down_hbm, down), (text_hbm, text))):
        copy = pltpu.make_async_copy(src, dst, load.at[number + 1])
        copy.start()
        loads.append(copy)
    partner = device(shifted(at, "k", 1))
    greet([device(shifted(at, axis, by)) for axis in "xyz" for by in (1, -1)] + [partner])
    own.wait()

    def slab_of(axes_done, axis, first, count):
        def slab(coordinate, half):
            cut = {name: (pl.ds(0, 4) if name in axes_done else pl.ds(at[name], 1)) for name in "xyz"}
            cut[axis] = pl.ds(coordinate, 1)
            return weight6.at[cut["x"], cut["z"], cut["y"], k, pl.ds(32 * half, 32), pl.ds(first, count)]

        return slab

    weight6 = weight.reshape(4, 4, 4, 2, 64, 1024)
    rings = [
        [
            Ring(at, order[phase], slab_of(order[:phase], order[phase], first, count), send, recv, (part * 3 + phase) * 6)
            for phase in range(3)
        ]
        for part, (first, count, order) in enumerate(PARTS)
    ]
    forwards = [{} for _ in PARTS]

    def forward(ref, number):
        copy = remote(ref, ref, forward_send.at[number], forward_recv.at[number], partner)
        copy.start()
        forwards[number // 7][number % 7] = copy

    for part in rings:
        part[0].start()

    loads[0].wait()
    vg = vit_gain[...].reshape(1, 1280)

    def norm_rows(step, carry):
        rows = pl.ds(pl.multiple_of(step * 16, 16), 16)
        for piece in range(4):
            columns = pl.ds(piece * 1280, 1280)
            value = patches[rows, columns].astype(F32)
            center = value - jnp.mean(value, axis=-1, keepdims=True)
            spread = jnp.mean(center * center, axis=-1, keepdims=True)
            patches[rows, columns] = (center * lax.rsqrt(spread + EPS) * vg).astype(BF)
        return carry

    lax.fori_loop(0, 16, norm_rows, 0)
    for part in rings:
        part[0].relay()

    loads[1].wait()
    inner[...] = jnp.zeros_like(inner)

    def up_step(step, carry):
        columns = pl.ds(pl.multiple_of(step * 1024, 1024), 1024)
        inner[...] += jnp.dot(patches[:, columns], up[columns, :], preferred_element_type=F32)
        return carry

    lax.fori_loop(0, 5, up_step, 0)
    for part in rings:
        for number in (2, 3, 4, 5):
            part[0].arrived(number)
        part[1].start()
    value = inner[...]
    hidden[...] = (0.5 * value * (1.0 + lax.erf(value * (1.0 / math.sqrt(2.0))))).astype(BF)
    loads[2].wait()

    width = 2048
    swaps = {}
    for chunk in ORDER:
        def down_step(step, carry, chunk=chunk):
            columns = pl.ds(pl.multiple_of(chunk * width + step * 512, 512), 512)
            product = jnp.dot(hidden[...], down[:, columns], preferred_element_type=F32)
            partial[:, :, :, columns] = product.astype(BF).reshape(4, 2, 32, 512)
            return carry

        lax.fori_loop(0, 4, down_step, 0)
        columns = pl.ds(chunk * width, width)
        swaps[chunk] = remote(
            partial.at[:, 1 - k, :, columns], from_partner.at[:, :, columns], pair_send.at[chunk], pair_recv.at[chunk], partner
        )
        swaps[chunk].start()
        if chunk == 2:
            for part in rings:
                part[1].relay()
    ring_sum = RingSum(at, sums, far, plain, through, 4, sum_send, sum_recv)
    for chunk in ORDER:
        swaps[chunk].wait_recv()
        columns = pl.ds(chunk * width, width)
        for block in range(4):
            mine = partial[block, pl.ds(k, 1), :, columns].reshape(32, width)
            sums[block, :, columns] = (mine.astype(F32) + from_partner[block, :, columns].astype(F32)).astype(BF)
        ring_sum.start(chunk)
    for number, part in enumerate(rings):
        for arrival in (2, 3, 4, 5):
            part[1].arrived(arrival)
        part[2].start()
        order = PARTS[number][2]
        cut = {name: (pl.ds(at[name], 1) if name == order[2] else pl.ds(0, 4)) for name in "xyz"}
        forward(weight6.at[cut["x"], cut["z"], cut["y"], k, :, pl.ds(PARTS[number][0], PARTS[number][1])], number * 7)

    loads[3].wait()

    def text_rows(step, carry):
        rows = pl.ds(pl.multiple_of(step * 16, 16), 16)
        value = text[rows, :].astype(F32)
        scale = lax.rsqrt(jnp.mean(value * value, axis=-1, keepdims=True) + EPS)
        normed[rows, :] = (value * scale * gain[...]).astype(BF)
        scales[rows, :] = jnp.broadcast_to(scale, (16, 128))
        return carry

    lax.fori_loop(0, 8, text_rows, 0)
    for chunk in ORDER:
        ring_sum.relay(chunk)
    for number, part in enumerate(rings):
        first, second = part[2].relay()
        forward(first, number * 7 + 1)
        forward(second, number * 7 + 2)
    for number, part in enumerate(rings):
        for arrival in (2, 3):
            forward(part[2].arrived(arrival), number * 7 + 1 + arrival)
    for chunk in ORDER:
        visual_out[:, pl.ds(chunk * width, width)] = ring_sum.total(chunk).astype(BF)
    for step in range(2):
        rows = pl.ds(step * 16, 16)
        value = visual_out[rows, :].astype(F32)
        scale = lax.rsqrt(jnp.mean(value * value, axis=-1, keepdims=True) + EPS)
        normed[pl.ds(128 + step * 16, 16), :] = (value * scale * gain[...]).astype(BF)
        scales[pl.ds(128 + step * 16, 16), :] = jnp.broadcast_to(scale, (16, 128))
    stores = []
    out6 = weight_out.reshape(4, 4, 4, 2, 64, 1024)

    def keep(step, numbers):
        for number, (first, count, order) in enumerate(PARTS):
            for each in numbers:
                forwards[number][each].wait_recv()
            spot = shifted(at, order[2], step)[order[2]]
            cut = {name: (pl.ds(spot, 1) if name == order[2] else pl.ds(0, 4)) for name in "xyz"}
            boxes = [
                ref.at[cut["x"], cut["z"], cut["y"], :, :, pl.ds(first, count)] for ref in (weight6, out6)
            ]
            copy = pltpu.make_async_copy(boxes[0], boxes[1], store.at[len(stores)])
            copy.start()
            stores.append(copy)

    keep(0, (0,))
    for number, part in enumerate(rings):
        for arrival in (4, 5):
            forward(part[2].arrived(arrival), number * 7 + 1 + arrival)
    keep(-1, (1, 3))
    keep(1, (2, 4))
    keep(2, (5, 6))
    acc[...] = jnp.zeros_like(acc)

    def project(step, carry):
        columns = pl.ds(pl.multiple_of(step * 2048, 2048), 2048)
        block = weight[pl.ds(step * 16, 16)].reshape(2048, 1024)
        acc[...] += jnp.dot(normed[:, columns], block, preferred_element_type=F32)
        return carry

    lax.fori_loop(0, 4, project, 0)
    text_pairs[...] = acc[pl.ds(0, 128), :].astype(BF)
    mine = acc[pl.ds(128, 32), :].astype(BF)
    visual_pairs[...] = mine
    entry = dest[...].reshape(1, 32)
    row_of = jnp.broadcast_to(upright(entry % 128 + 1), (32, 128)).astype(BF)
    picking = (lax.broadcasted_iota(jnp.int32, (128, 32), 0) == entry // 128).astype(F32).astype(BF)
    outgoing[:, :, pl.ds(0, 1024)] = jnp.dot(picking, mine, preferred_element_type=F32).reshape(16, 8, 1024).astype(BF)
    outgoing[:, :, pl.ds(1024, 128)] = jnp.dot(picking, row_of, preferred_element_type=F32).reshape(16, 8, 128).astype(BF)
    for part in rings:
        for ring in part:
            ring.finish()
    for part in forwards:
        for copy in part.values():
            copy.wait_send()
    for chunk in ORDER:
        swaps[chunk].wait_send()
    ring_sum.finish()
    for copy in stores:
        copy.wait()


def first_call(patches, vit_gain, up, down, text, gain, kv, dest):
    shape = jax.ShapeDtypeStruct
    dma = pltpu.SemaphoreType.DMA
    return pl.pallas_call(
        first_kernel,
        out_shape=(
            shape((64, 2, 64, 1024), BF), shape((16, 8, 1152), BF), shape((128, 1024), BF), shape((32, 1024), BF),
            shape((32, 8192), BF), shape((160, 128), F32),
        ),
        in_specs=[ANY, VM, ANY, ANY, ANY, VM, ANY, VM],
        out_specs=(ANY, VM, VM, VM, VM, VM),
        scratch_shapes=[
            pltpu.VMEM((64, 2, 64, 1024), BF), pltpu.VMEM((256, 5120), BF), pltpu.VMEM((5120, 384), BF),
            pltpu.VMEM((384, 8192), BF), pltpu.VMEM((128, 8192), BF), pltpu.VMEM((160, 8192), BF), pltpu.VMEM((256, 384), BF),
            pltpu.VMEM((4, 2, 32, 8192), BF), pltpu.VMEM((4, 32, 8192), BF), pltpu.VMEM((4, 32, 8192), BF),
            pltpu.VMEM((4, 32, 2048), BF), pltpu.VMEM((4, 32, 2048), BF), pltpu.VMEM((4, 32, 2048), BF),
            pltpu.VMEM((160, 1024), F32), pltpu.VMEM((256, 384), F32),
            dma((6,)), dma((54,)), dma((54,)), dma((21,)), dma((21,)), dma((4,)), dma((4,)), dma((12,)), dma((12,)), dma((12,)),
        ],
        compiler_params=pltpu.CompilerParams(collective_id=1, has_side_effects=True, vmem_limit_bytes=62 * 2**20),
        name="merge_and_project",
    )(patches, vit_gain, up, down, text, gain, kv, dest)


def exchange_kernel(
    outgoing, text_pairs, weight, text_all, visual_all, placing, marked, weight_t,
    landed, turned, arrived, block, block_t,
    load, store, ctx_send, ctx_recv, dp_send, dp_recv, send, recv, forward_send, forward_recv,
):
    at = place()
    dp, ctx = lax.axis_index("dp"), lax.axis_index("ctx")
    k, y = at["k"], at["y"]
    own = pltpu.make_async_copy(text_pairs, text_all.at[y, k], load.at[2])
    own.start()
    fetched, stored = [], []

    def fetch(chunk):
        copy = pltpu.make_async_copy(weight.at[pl.ds(chunk * 1024, 1024)], block.at[chunk % 2], load.at[3 + chunk])
        copy.start()
        fetched.append(copy)

    def transpose(chunk):
        fetched[chunk].wait()
        if chunk >= 2:
            stored[chunk - 2].wait()

        def step(i, carry):
            lanes = pl.ds(pl.multiple_of(i * 128, 128), 128)
            block_t[chunk % 2, :, lanes] = block[chunk % 2, lanes, :].T
            return carry

        lax.fori_loop(0, 8, step, 0)
        copy = pltpu.make_async_copy(block_t.at[chunk % 2], weight_t.at[:, pl.ds(chunk * 1024, 1024)], store.at[chunk])
        copy.start()
        stored.append(copy)
        if chunk + 2 < 8:
            fetch(chunk + 2)

    fetch(0)
    fetch(1)
    greet([(dp, lax.rem(ctx + by, 8)) for by in range(1, 8)] + [(lax.rem(dp + by, 16), ctx) for by in range(1, 16)])
    partner = device(shifted(at, "k", 1))
    text_ring = Ring(at, "y", lambda coordinate, half: text_all.at[coordinate, k, pl.ds(64 * half, 64)], send, recv, 0)
    visual_ring = Ring(at, "y", lambda coordinate, half: visual_all.at[coordinate, k, pl.ds(16 * half, 16)], send, recv, 6)
    forwards, copies = [], []

    def forward(ref, number):
        copy = remote(ref, ref, forward_send.at[number], forward_recv.at[number], partner)
        copy.start()
        forwards.append(copy)

    for by in range(1, 16):
        to = lax.rem(dp + by, 16)
        copy = remote(outgoing.at[to], landed.at[dp], dp_send.at[by - 1], dp_recv.at[by - 1], (to, ctx))
        copy.start()
        copies.append(copy)
    own.wait()
    text_ring.start()
    forward(text_all.at[y, k], 0)
    own = pltpu.make_async_copy(outgoing.at[dp], landed.at[dp], load.at[0])
    own.start()
    transpose(0)
    transpose(1)
    first, second = text_ring.relay()
    forward(first, 1)
    forward(second, 2)
    own.wait()
    for by in range(1, 16):
        source = lax.rem(dp - by + 16, 16)
        remote(landed.at[source], landed.at[source], dp_send.at[by - 1], dp_recv.at[by - 1], (source, ctx)).wait_recv()
    row = lax.broadcasted_iota(jnp.int32, (128, 128), 0)
    turn = (lax.broadcasted_iota(jnp.int32, (128, 128), 1) == (row % 16) * 8 + row // 16).astype(F32).astype(BF)
    came = landed[...].astype(F32).reshape(128, 1152).astype(BF)
    turned[...] = jnp.dot(turn, came, preferred_element_type=F32).astype(BF).reshape(8, 16, 1152)
    for by in range(1, 8):
        to = lax.rem(ctx + by, 8)
        copy = remote(turned.at[to], arrived.at[ctx], ctx_send.at[by - 1], ctx_recv.at[by - 1], (dp, to))
        copy.start()
        copies.append(copy)
    own = pltpu.make_async_copy(turned.at[ctx], arrived.at[ctx], load.at[1])
    own.start()
    transpose(2)
    transpose(3)
    own.wait()
    for by in range(1, 8):
        source = lax.rem(ctx - by + 8, 8)
        remote(arrived.at[source], arrived.at[source], ctx_send.at[by - 1], ctx_recv.at[by - 1], (dp, source)).wait_recv()
    rows = arrived[:, :, pl.ds(1024, 128)].astype(F32).reshape(128, 128)
    lane = lax.broadcasted_iota(jnp.int32, (128, 128), 1).astype(F32)
    contract = (((0,), (0,)), ((), ()))
    begin = jnp.min(jnp.where(rows > 0.5, rows, 1000.0), axis=0, keepdims=True)
    packing = (rows - begin == lane).astype(F32).astype(BF)
    packed = lax.dot_general(
        packing, arrived[:, :, pl.ds(0, 1024)].reshape(128, 1024), contract, preferred_element_type=F32
    )
    visual_all[y, k, :, pl.ds(0, 1024)] = packed[:32].astype(BF)
    visual_all[y, k, :, pl.ds(1024, 128)] = jnp.broadcast_to(begin, (32, 128)).astype(BF)
    visual_ring.start()
    forward(visual_all.at[y, k], 7)
    places = (rows == lane + 1.0).astype(F32).astype(BF)
    placing[...] = places
    marked[...] = lax.dot_general(places, jnp.ones((128, 128), BF), contract, preferred_element_type=F32)
    transpose(4)
    for number in (2, 3, 4, 5):
        forward(text_ring.arrived(number), number + 1)
    first, second = visual_ring.relay()
    forward(first, 8)
    forward(second, 9)
    transpose(5)
    for number in (2, 3):
        forward(visual_ring.arrived(number), number + 8)
    transpose(6)
    for number in (4, 5):
        forward(visual_ring.arrived(number), number + 8)
    transpose(7)
    for copy in forwards:
        copy.wait()
    for copy in copies:
        copy.wait_send()
    text_ring.finish()
    visual_ring.finish()
    stored[6].wait()
    stored[7].wait()


def exchange_call(outgoing, text_pairs, weight):
    shape = jax.ShapeDtypeStruct
    dma = pltpu.SemaphoreType.DMA
    return pl.pallas_call(
        exchange_kernel,
        out_shape=(
            shape((4, 2, 128, 1024), BF), shape((4, 2, 32, 1152), BF), shape((128, 128), BF), shape((128, 128), F32),
            shape((1024, 8192), BF),
        ),
        in_specs=[ANY, ANY, ANY],
        out_specs=(VM, VM, VM, VM, ANY),
        scratch_shapes=[
            pltpu.VMEM((16, 8, 1152), BF), pltpu.VMEM((8, 16, 1152), BF), pltpu.VMEM((8, 16, 1152), BF),
            pltpu.VMEM((2, 1024, 1024), BF), pltpu.VMEM((2, 1024, 1024), BF),
            dma((11,)), dma((8,)), dma((7,)), dma((7,)), dma((15,)), dma((15,)), dma((12,)), dma((12,)), dma((14,)), dma((14,)),
        ],
        compiler_params=pltpu.CompilerParams(collective_id=2, has_side_effects=True, vmem_limit_bytes=62 * 2**20),
        name="exchange_pairs",
    )(outgoing, text_pairs, weight)


WINDOWS = (2, 3, 4, 5)


def attend_kernel(assign, own, text_all, visual_all, docs, queries, upstream, attn_out, q_grad, pair_grads, held, turned):
    head = pl.program_id(0)

    @pl.when(head == 0)
    def _():
        row = lax.broadcasted_iota(jnp.int32, (128, 32), 0)
        column = lax.broadcasted_iota(jnp.int32, (128, 32), 1)

        def fill(source, carry):
            begin = visual_all[source, 0:1, 1024:1025].astype(F32).astype(jnp.int32) - 1
            spread = (row - column == begin).astype(F32).astype(BF)
            placed = jnp.dot(spread, visual_all[source, :, 0:1024], preferred_element_type=F32)
            inside = (row[:, 0:1] >= begin) & (row[:, 0:1] < begin + 32)
            both = jnp.where(inside, placed, text_all[source].astype(F32)).astype(BF)
            held[assign[2 * source]] = both[:64]
            held[assign[2 * source + 1]] = both[64:]
            return carry

        lax.fori_loop(0, 8, fill, 0)

    labels = docs[...]
    starts = [jnp.sum((labels < d).astype(F32)).astype(jnp.int32) for d in (1, 2, 3)]
    key_columns = pl.ds(pl.multiple_of(head * HD, HD), HD)
    value_columns = pl.ds(pl.multiple_of(KVH * HD + head * HD, HD), HD)
    turned[...] = jnp.zeros_like(turned)
    score_scale = HD**-0.5
    outer = (((0,), (0,)), ((), ()))
    inner = (((1,), (1,)), ((), ()))

    def attend(half, position, chunks):
        window = chunks * 128
        low = jnp.maximum(position // 2 - (chunks - 1), 0)
        rows = pl.ds(pl.multiple_of(half * 64, 64), 64)
        query = jnp.concatenate([queries[rows, g * HD : (g + 1) * HD] for g in range(GROUP)], axis=0)
        grad = jnp.concatenate([upstream[rows, g * HD : (g + 1) * HD] for g in range(GROUP)], axis=0)
        blocks = pl.ds(low * 2, window // 64)
        keys = held[blocks, :, key_columns].reshape(window, HD)
        values = held[blocks, :, value_columns].reshape(window, HD)
        query_at = position * 64 + lax.broadcasted_iota(jnp.int32, (64, window), 0)
        key_at = low * 128 + lax.broadcasted_iota(jnp.int32, (64, window), 1)
        begin = jnp.zeros((64, window), jnp.int32)
        for start in starts:
            begin = jnp.where(query_at >= start, start, begin)
        allowed = (key_at <= query_at) & (key_at >= begin)
        scores = lax.dot_general(query, keys, inner, preferred_element_type=F32).reshape(GROUP, 64, window)
        scores = jnp.where(allowed[None], scores * (score_scale * math.log2(math.e)), -1e30)
        weights = jnp.exp2(scores - jnp.max(scores, axis=-1, keepdims=True))
        weights = weights * (1.0 / jnp.sum(weights, axis=-1, keepdims=True))
        weights = weights.reshape(GROUP * 64, window)
        light = weights.astype(BF)
        output = jnp.dot(light, values, preferred_element_type=F32)
        weight_grad = lax.dot_general(grad, values, inner, preferred_element_type=F32)
        inner_sum = jnp.sum(weights * weight_grad, axis=-1, keepdims=True)
        score_grad = (weights * (weight_grad - inner_sum)).astype(BF)
        query_grad = jnp.dot(score_grad, keys, preferred_element_type=F32) * score_scale
        window_at = pl.ds(pl.multiple_of(low * 128, 128), window)
        turned[0, :, window_at] += lax.dot_general(query, score_grad, outer, preferred_element_type=F32)
        turned[1, :, window_at] += lax.dot_general(grad, light, outer, preferred_element_type=F32)
        for g in range(GROUP):
            attn_out[rows, g * HD : (g + 1) * HD] = output[g * 64 : (g + 1) * 64].astype(BF)
            q_grad[rows, g * HD : (g + 1) * HD] = query_grad[g * 64 : (g + 1) * 64].astype(BF)

    def one_half(half, carry):
        position = assign[own[0] * 2 + half]
        begin = jnp.int32(0)
        for start in starts:
            begin = jnp.where(position * 64 >= start, start, begin)
        need = position // 2 - begin // 128 + 1
        for chunks in WINDOWS:
            fits = need <= chunks if chunks == WINDOWS[0] else need == chunks

            @pl.when(fits)
            def _(chunks=chunks):
                attend(half, position, chunks)

        return carry

    lax.fori_loop(0, 2, one_half, 0)
    held[:, :, key_columns] = (turned[0] * score_scale).T.reshape(16, 64, HD).astype(BF)
    held[:, :, value_columns] = turned[1].T.reshape(16, 64, HD).astype(BF)
    for block in range(16):
        pair_grads[block, :, key_columns] = held[assign[block], :, key_columns]
        pair_grads[block, :, value_columns] = held[assign[block], :, value_columns]


def attend_call(assign, own, text_all, visual_all, docs, queries, upstream):
    shape = jax.ShapeDtypeStruct
    by_head = pl.BlockSpec((128, GROUP * HD), lambda head, *_: (0, head))

    def whole(*dims):
        return pl.BlockSpec(dims, lambda head, *_: (0,) * len(dims))

    return pl.pallas_call(
        attend_kernel,
        out_shape=(shape((128, 4096), BF), shape((128, 4096), BF), shape((16, 64, 1024), BF)),
        grid_spec=pltpu.PrefetchScalarGridSpec(
            num_scalar_prefetch=2,
            grid=(KVH,),
            in_specs=[whole(8, 128, 1024), whole(8, 32, 1152), whole(1, 1024), by_head, by_head],
            out_specs=(by_head, by_head, whole(16, 64, 1024)),
            scratch_shapes=[pltpu.VMEM((16, 64, 1024), BF), pltpu.VMEM((2, HD, 1024), F32)],
        ),
        compiler_params=pltpu.CompilerParams(vmem_limit_bytes=50 * 2**20),
        name="attend",
    )(assign, own, text_all, visual_all, docs, queries, upstream)


def return_kernel(
    grads, placing, dest, own_grad, visual_grad,
    from_partner, sums, far, plain, through, leaving, landed, turned, arrived,
    load, pair_send, pair_recv, sum_send, sum_recv, dp_send, dp_recv, ctx_send, ctx_recv,
):
    at = place()
    dp, ctx = lax.axis_index("dp"), lax.axis_index("ctx")
    k, y = at["k"], at["y"]
    greet([(dp, lax.rem(ctx + by, 8)) for by in range(1, 8)] + [(lax.rem(dp + by, 16), ctx) for by in range(1, 16)])
    partner = device(shifted(at, "k", 1))
    width = 256
    swaps = {}
    for chunk in ORDER:
        columns = pl.ds(chunk * width, width)
        swaps[chunk] = remote(
            grads.at[:, 1 - k, :, columns], from_partner.at[:, :, columns], pair_send.at[chunk], pair_recv.at[chunk], partner
        )
        swaps[chunk].start()
    ring_sum = RingSum(at, sums, far, plain, through, 4, sum_send, sum_recv)
    for chunk in ORDER:
        swaps[chunk].wait_recv()
        columns = pl.ds(chunk * width, width)
        for block in range(4):
            mine = grads[block, pl.ds(k, 1), :, columns].reshape(128, width)
            sums[block, :, columns] = (mine.astype(F32) + from_partner[block, :, columns].astype(F32)).astype(BF)
        ring_sum.start(chunk)
    for chunk in ORDER:
        ring_sum.relay(chunk)
    for chunk in ORDER:
        own_grad[:, pl.ds(chunk * width, width)] = ring_sum.total(chunk).astype(BF)
    leaving[...] = jnp.dot(placing[...], own_grad[...], preferred_element_type=F32).astype(BF).reshape(8, 16, 1024)
    own = pltpu.make_async_copy(leaving.at[ctx], landed.at[ctx], load.at[0])
    own.start()
    copies = []
    for by in range(1, 8):
        to = lax.rem(ctx + by, 8)
        copy = remote(leaving.at[to], landed.at[ctx], ctx_send.at[by - 1], ctx_recv.at[by - 1], (dp, to))
        copy.start()
        copies.append(copy)
    own.wait()
    for by in range(1, 8):
        source = lax.rem(ctx - by + 8, 8)
        remote(landed.at[source], landed.at[source], ctx_send.at[by - 1], ctx_recv.at[by - 1], (dp, source)).wait_recv()
    row = lax.broadcasted_iota(jnp.int32, (128, 128), 0)
    turn = (lax.broadcasted_iota(jnp.int32, (128, 128), 1) == (row % 8) * 16 + row // 8).astype(F32).astype(BF)
    turned[...] = jnp.dot(turn, landed[...].reshape(128, 1024), preferred_element_type=F32).reshape(16, 8, 1024).astype(BF)
    for by in range(1, 16):
        to = lax.rem(dp + by, 16)
        copy = remote(turned.at[to], arrived.at[dp], dp_send.at[by - 1], dp_recv.at[by - 1], (to, ctx))
        copy.start()
        copies.append(copy)
    own = pltpu.make_async_copy(turned.at[dp], arrived.at[dp], load.at[1])
    own.start()
    own.wait()
    for by in range(1, 16):
        source = lax.rem(dp - by + 16, 16)
        remote(arrived.at[source], arrived.at[source], dp_send.at[by - 1], dp_recv.at[by - 1], (source, ctx)).wait_recv()
    target = jnp.broadcast_to(upright(dest[...].reshape(1, 32) // 128), (32, 128))
    picking = (target == lax.broadcasted_iota(jnp.int32, (32, 128), 1).astype(F32)).astype(F32).astype(BF)
    came = arrived[...].astype(F32).reshape(128, 1024).astype(BF)
    visual_grad[...] = jnp.dot(picking, came, preferred_element_type=F32).astype(BF)
    for copy in copies:
        copy.wait_send()
    for chunk in ORDER:
        swaps[chunk].wait_send()
    ring_sum.finish()


def return_call(grads, placing, dest):
    shape = jax.ShapeDtypeStruct
    dma = pltpu.SemaphoreType.DMA
    return pl.pallas_call(
        return_kernel,
        out_shape=(shape((128, 1024), BF), shape((32, 1024), BF)),
        in_specs=[VM, VM, VM],
        out_specs=(VM, VM),
        scratch_shapes=[
            pltpu.VMEM((4, 128, 1024), BF), pltpu.VMEM((4, 128, 1024), BF),
            pltpu.VMEM((4, 128, 256), BF), pltpu.VMEM((4, 128, 256), BF), pltpu.VMEM((4, 128, 256), BF),
            pltpu.VMEM((8, 16, 1024), BF), pltpu.VMEM((8, 16, 1024), BF), pltpu.VMEM((16, 8, 1024), BF), pltpu.VMEM((16, 8, 1024), BF),
            dma((2,)), dma((4,)), dma((4,)), dma((12,)), dma((12,)), dma((15,)), dma((15,)), dma((7,)), dma((7,)),
        ],
        compiler_params=pltpu.CompilerParams(collective_id=3, has_side_effects=True, vmem_limit_bytes=50 * 2**20),
        name="return_grads",
    )(grads, placing, dest)


def final_kernel(
    own_grad, visual_pair_grad, text_pairs, visual_pairs, weight, text, visual, gain, scales, marked, hidden_grad, visual_grad
):
    block = weight[...]
    gains = gain[...]

    def through(grad, pair, value, scale):
        mean = jnp.sum(grad.astype(F32) * pair.astype(F32), axis=-1, keepdims=True) * (1.0 / 8192.0)
        normed_grad = jnp.dot(grad, block, preferred_element_type=F32)
        return scale * (gains * normed_grad) - value.astype(F32) * (scale * scale * mean)

    full = through(own_grad[...], text_pairs[...], text[...], scales[0:128, 0:1])
    hidden_grad[...] = jnp.where(marked[:, 0:1] > 0.5, 0.0, full).astype(BF)
    visual_grad[...] = through(visual_pair_grad[...], visual_pairs[...], visual[...], scales[128:160, 0:1]).astype(BF)


def final_call(own_grad, visual_pair_grad, text_pairs, visual_pairs, weight, text, visual, gain, scales, marked):
    shape = jax.ShapeDtypeStruct
    tile = 1024

    def whole(*dims):
        return pl.BlockSpec(dims, lambda i: (0,) * len(dims))

    return pl.pallas_call(
        final_kernel,
        out_shape=(shape((128, 8192), BF), shape((32, 8192), BF)),
        grid=(8192 // tile,),
        in_specs=[
            whole(128, 1024), whole(32, 1024), whole(128, 1024), whole(32, 1024),
            pl.BlockSpec((1024, tile), lambda i: (0, i)), pl.BlockSpec((128, tile), lambda i: (0, i)),
            pl.BlockSpec((32, tile), lambda i: (0, i)), pl.BlockSpec((1, tile), lambda i: (0, i)),
            whole(160, 128), whole(128, 128),
        ],
        out_specs=(pl.BlockSpec((128, tile), lambda i: (0, i)), pl.BlockSpec((32, tile), lambda i: (0, i))),
        compiler_params=pltpu.CompilerParams(vmem_limit_bytes=52 * 2**20),
        name="through_norm",
    )(own_grad, visual_pair_grad, text_pairs, visual_pairs, weight, text, visual, gain, scales, marked)


def local(patches, vit_gain, merge_up, merge_down, dest, text, norm_gain, kv_weight, queries, out_grad, assign, docs):
    gain = norm_gain.reshape(1, 8192)
    weight, outgoing, text_pairs, visual_pairs, visual, scales = first_call(
        patches, vit_gain, merge_up, merge_down, text[0], gain, kv_weight, dest
    )
    text_all, visual_all, placing, marked, weight_t = exchange_call(outgoing, text_pairs, weight.reshape(8192, 1024))
    own = lax.axis_index("ctx").astype(jnp.int32).reshape(1)
    attention, query_grad, pair_grads = attend_call(
        assign, own, text_all.reshape(8, 128, 1024), visual_all.reshape(8, 32, 1152), docs, queries[0], out_grad[0]
    )
    own_grad, visual_pair_grad = return_call(pair_grads.reshape(4, 2, 128, 1024), placing, dest)
    hidden_grad, visual_grad = final_call(
        own_grad, visual_pair_grad, text_pairs, visual_pairs, weight_t, text[0], visual, gain, scales, marked
    )
    return attention[None], query_grad[None], hidden_grad[None], visual_grad


def solution(mesh):
    placed = (
        P("dp", None),
        P(),
        P(None, "ctx"),
        P("ctx", None),
        P(("dp", "ctx")),
        P("dp", "ctx", None),
        P(),
        P(("dp", "ctx"), None),
        P("dp", "ctx", None),
        P("dp", "ctx", None),
        P(),
        P("dp", None),
    )
    return jax.shard_map(
        local,
        mesh=mesh,
        in_specs=placed,
        out_specs=(P("dp", "ctx", None), P("dp", "ctx", None), P("dp", "ctx", None), P(("dp", "ctx"), None)),
        check_vma=False,
    )
```

```python
import functools
import math

import jax
import jax.numpy as jnp
from jax import lax
from jax.experimental import pallas as pl
from jax.experimental.pallas import tpu as pltpu
from jax.sharding import PartitionSpec as P

MESH = pl.DeviceIdType.MESH
BF = jnp.bfloat16
F32 = jnp.float32
HEADS = 32
KVH = 4
HD = 128
GROUP = HEADS // KVH
EPS = 1e-06
VMEM_ALL = 67043328
ANY = pl.BlockSpec(memory_space=pl.ANY)
VM = pl.BlockSpec(memory_space=pltpu.VMEM)


def place():
    dp, ctx = lax.axis_index("dp"), lax.axis_index("ctx")
    return {"x": dp // 4, "z": dp % 4, "y": ctx // 2, "k": ctx % 2}


def device(at):
    return (at["x"] * 4 + at["z"], at["y"] * 2 + at["k"])


def shifted(at, axis, by):
    size = 2 if axis == "k" else 4
    return dict(at, **{axis: lax.rem(at[axis] + by + size, size)})


def remote(src, dst, send, recv, to):
    return pltpu.make_async_remote_copy(
        src_ref=src, dst_ref=dst, send_sem=send, recv_sem=recv, device_id=to, device_id_type=MESH
    )


def greet(devices):
    barrier = pltpu.get_barrier_semaphore()
    for to in devices:
        pl.semaphore_signal(barrier, inc=1, device_id=to, device_id_type=MESH)
    pl.semaphore_wait(barrier, len(devices))


def upright(row):
    same = lax.broadcasted_iota(jnp.int32, (32, 32), 0) == lax.broadcasted_iota(jnp.int32, (32, 32), 1)
    return jnp.sum(jnp.where(same, jnp.broadcast_to(row, (32, 32)), 0).astype(F32), axis=1, keepdims=True)


class Ring:
    def __init__(self, at, axis, slab, send, recv, base):
        self.at, self.axis, self.slab, self.send, self.recv, self.base = at, axis, slab, send, recv, base
        self.plus, self.minus = device(shifted(at, axis, 1)), device(shifted(at, axis, -1))
        self.sent = []

    def _coordinate(self, by):
        return shifted(self.at, self.axis, by)[self.axis]

    def _copy(self, by, half, number, to):
        ref = self.slab(self._coordinate(by), half)
        copy = remote(ref, ref, self.send.at[self.base + number], self.recv.at[self.base + number], to)
        copy.start()
        self.sent.append(copy)

    def start(self):
        self._copy(0, 0, 0, self.plus)
        self._copy(0, 1, 1, self.minus)
        self._copy(0, 1, 2, self.plus)
        self._copy(0, 0, 3, self.minus)

    ARRIVALS = ((-1, 0), (1, 1), (-1, 1), (1, 0), (2, 0), (2, 1))

    def arrived(self, number):
        by, half = self.ARRIVALS[number]
        ref = self.slab(self._coordinate(by), half)
        remote(ref, ref, self.send.at[self.base + number], self.recv.at[self.base + number], self.plus).wait_recv()
        return ref

    def relay(self):
        first, second = self.arrived(0), self.arrived(1)
        self._copy(-1, 0, 4, self.plus)
        self._copy(1, 1, 5, self.minus)
        return first, second

    def finish(self):
        for copy in self.sent:
            copy.wait_send()


class RingSum:
    def __init__(self, at, sums, far, plain, through, chunks, send, recv):
        self.at, self.sums, self.far, self.plain, self.through = at, sums, far, plain, through
        self.chunks, self.send, self.recv = chunks, send, recv
        self.width = sums.shape[2] // chunks
        self.sent = []

    def _block(self, by, chunk):
        y = shifted(self.at, "y", by)["y"]
        return self.sums.at[y, :, pl.ds(chunk * self.width, self.width)]

    def _way(self, chunk):
        return 1 if chunk < self.chunks // 2 else -1

    def _copy(self, src, dst, number, by):
        copy = remote(src, dst, self.send.at[number], self.recv.at[number], device(shifted(self.at, "y", by)))
        copy.start()
        self.sent.append(copy)

    def _wait(self, dst, number):
        remote(dst, dst, self.send.at[number], self.recv.at[number], device(shifted(self.at, "y", 1))).wait_recv()

    def start(self, chunk):
        way = self._way(chunk)
        self._copy(self._block(2, chunk), self.far.at[chunk], chunk * 3, way)
        self._copy(self._block(-way, chunk), self.plain.at[chunk], chunk * 3 + 1, -way)

    def relay(self, chunk):
        way = self._way(chunk)
        self._wait(self.far.at[chunk], chunk * 3)
        block = self._block(way, chunk)
        block[...] = (block[...].astype(F32) + self.far[chunk].astype(F32)).astype(BF)
        self._copy(block, self.through.at[chunk], chunk * 3 + 2, way)

    def total(self, chunk):
        self._wait(self.plain.at[chunk], chunk * 3 + 1)
        self._wait(self.through.at[chunk], chunk * 3 + 2)
        own = self._block(0, chunk)[...].astype(F32)
        return own + self.plain[chunk].astype(F32) + self.through[chunk].astype(F32)

    def finish(self):
        for copy in self.sent:
            copy.wait_send()


PARTS = ((0, 384, "yzx"), (384, 384, "xyz"), (768, 256, "zxy"))
STEPS = (0, -1, 1, 2)
ORDER = (0, 2, 1, 3)


def first_kernel(
    patches_hbm, vit_gain, up_hbm, down_hbm, text_hbm, gain, kv_hbm, dest,
    text_all, visual_all, placing, marked, weight_t, text_pairs, visual_pairs, visual_out, scales,
    weight, patches, up, down, text, normed, hidden, partial, from_partner, sums, far, plain, through, acc, inner,
    outgoing, landed, turned, arrived, block_t,
    load, send, recv, forward_send, forward_recv, pair_send, pair_recv, sum_send, sum_recv, store,
    ctx_send, ctx_recv, dp_send, dp_recv,
):
    at = place()
    k, y = at["k"], at["y"]
    chip = (at["x"] * 4 + at["z"]) * 4 + y
    own = pltpu.make_async_copy(kv_hbm, weight.at[chip, k], load.at[0])
    own.start()
    loads = []
    for number, (src, dst) in enumerate(((patches_hbm, patches), (up_hbm, up), (down_hbm, down), (text_hbm, text))):
        copy = pltpu.make_async_copy(src, dst, load.at[number + 1])
        copy.start()
        loads.append(copy)
    partner = device(shifted(at, "k", 1))
    dp, ctx = lax.axis_index("dp"), lax.axis_index("ctx")
    greet([(dp, lax.rem(ctx + by, 8)) for by in range(1, 8)] + [(lax.rem(dp + by, 16), ctx) for by in range(1, 16)])
    own.wait()

    def slab_of(axes_done, axis, first, count):
        def slab(coordinate, half):
            cut = {name: (pl.ds(0, 4) if name in axes_done else pl.ds(at[name], 1)) for name in "xyz"}
            cut[axis] = pl.ds(coordinate, 1)
            return weight6.at[cut["x"], cut["z"], cut["y"], k, pl.ds(32 * half, 32), pl.ds(first, count)]

        return slab

    weight6 = weight.reshape(4, 4, 4, 2, 64, 1024)
    rings = [
        [
            Ring(at, order[phase], slab_of(order[:phase], order[phase], first, count), send, recv, (part * 3 + phase) * 6)
            for phase in range(3)
        ]
        for part, (first, count, order) in enumerate(PARTS)
    ]
    forwards = [{} for _ in PARTS]

    def forward(ref, number):
        copy = remote(ref, ref, forward_send.at[number], forward_recv.at[number], partner)
        copy.start()
        forwards[number // 7][number % 7] = copy

    for part in rings:
        part[0].start()

    loads[0].wait()
    vg = vit_gain[...].reshape(1, 1280)

    def norm_rows(step, carry):
        rows = pl.ds(pl.multiple_of(step * 16, 16), 16)
        for piece in range(4):
            columns = pl.ds(piece * 1280, 1280)
            value = patches[rows, columns].astype(F32)
            center = value - jnp.mean(value, axis=-1, keepdims=True)
            spread = jnp.mean(center * center, axis=-1, keepdims=True)
            patches[rows, columns] = (center * lax.rsqrt(spread + EPS) * vg).astype(BF)
        return carry

    lax.fori_loop(0, 6, norm_rows, 0)
    for part in rings:
        part[0].relay()
    lax.fori_loop(6, 16, norm_rows, 0)
    for part in rings:
        for number in (2, 3, 4, 5):
            part[0].arrived(number)
        part[1].start()
    loads[1].wait()
    inner[...] = jnp.zeros_like(inner)

    def up_step(step, carry):
        columns = pl.ds(pl.multiple_of(step * 1024, 1024), 1024)
        inner[...] += jnp.dot(patches[:, columns], up[columns, :], preferred_element_type=F32)
        return carry

    lax.fori_loop(0, 5, up_step, 0)
    value = inner[...]
    hidden[...] = (0.5 * value * (1.0 + lax.erf(value * (1.0 / math.sqrt(2.0))))).astype(BF)
    loads[2].wait()

    width = 2048
    swaps = {}
    for chunk in ORDER:
        def down_step(step, carry, chunk=chunk):
            columns = pl.ds(pl.multiple_of(chunk * width + step * 512, 512), 512)
            product = jnp.dot(hidden[...], down[:, columns], preferred_element_type=F32)
            partial[:, :, :, columns] = product.astype(BF).reshape(4, 2, 32, 512)
            return carry

        lax.fori_loop(0, 4, down_step, 0)
        columns = pl.ds(chunk * width, width)
        swaps[chunk] = remote(
            partial.at[:, 1 - k, :, columns], from_partner.at[:, :, columns], pair_send.at[chunk], pair_recv.at[chunk], partner
        )
        swaps[chunk].start()
        if chunk == 2:
            for part in rings:
                part[1].relay()
    ring_sum = RingSum(at, sums, far, plain, through, 4, sum_send, sum_recv)
    for chunk in ORDER:
        swaps[chunk].wait_recv()
        columns = pl.ds(chunk * width, width)
        for block in range(4):
            mine = partial[block, pl.ds(k, 1), :, columns].reshape(32, width)
            sums[block, :, columns] = (mine.astype(F32) + from_partner[block, :, columns].astype(F32)).astype(BF)
        ring_sum.start(chunk)
    for number, part in enumerate(rings):
        for arrival in (2, 3, 4, 5):
            part[1].arrived(arrival)
        part[2].start()
        order = PARTS[number][2]
        cut = {name: (pl.ds(at[name], 1) if name == order[2] else pl.ds(0, 4)) for name in "xyz"}
        forward(weight6.at[cut["x"], cut["z"], cut["y"], k, :, pl.ds(PARTS[number][0], PARTS[number][1])], number * 7)

    loads[3].wait()

    def text_rows(step, carry):
        rows = pl.ds(pl.multiple_of(step * 16, 16), 16)
        value = text[rows, :].astype(F32)
        scale = lax.rsqrt(jnp.mean(value * value, axis=-1, keepdims=True) + EPS)
        normed[rows, :] = (value * scale * gain[...]).astype(BF)
        scales[rows, :] = jnp.broadcast_to(scale, (16, 128))
        return carry

    lax.fori_loop(0, 8, text_rows, 0)
    for chunk in ORDER:
        ring_sum.relay(chunk)
    for number, part in enumerate(rings):
        first, second = part[2].relay()
        forward(first, number * 7 + 1)
        forward(second, number * 7 + 2)
    for number, part in enumerate(rings):
        for arrival in (2, 3):
            forward(part[2].arrived(arrival), number * 7 + 1 + arrival)
    for chunk in ORDER:
        visual_out[:, pl.ds(chunk * width, width)] = ring_sum.total(chunk).astype(BF)
    for step in range(2):
        rows = pl.ds(step * 16, 16)
        value = visual_out[rows, :].astype(F32)
        scale = lax.rsqrt(jnp.mean(value * value, axis=-1, keepdims=True) + EPS)
        normed[pl.ds(128 + step * 16, 16), :] = (value * scale * gain[...]).astype(BF)
        scales[pl.ds(128 + step * 16, 16), :] = jnp.broadcast_to(scale, (16, 128))
    for number, part in enumerate(rings):
        for arrival in (4, 5):
            forward(part[2].arrived(arrival), number * 7 + 1 + arrival)
    for part in forwards:
        for copy in part.values():
            copy.wait_recv()
    acc[...] = jnp.zeros_like(acc)

    def project(step, carry):
        columns = pl.ds(pl.multiple_of(step * 2048, 2048), 2048)
        block = weight[pl.ds(step * 16, 16)].reshape(2048, 1024)
        acc[...] += jnp.dot(normed[:, columns], block, preferred_element_type=F32)
        return carry

    lax.fori_loop(0, 4, project, 0)
    text_pairs[...] = acc[pl.ds(0, 128), :].astype(BF)
    mine = acc[pl.ds(128, 32), :].astype(BF)
    visual_pairs[...] = mine
    entry = dest[...].reshape(1, 32)
    row_of = jnp.broadcast_to(upright(entry % 128 + 1), (32, 128)).astype(BF)
    picking = (lax.broadcasted_iota(jnp.int32, (128, 32), 0) == entry // 128).astype(F32).astype(BF)
    outgoing[:, :, pl.ds(0, 1024)] = jnp.dot(picking, mine, preferred_element_type=F32).reshape(16, 8, 1024).astype(BF)
    outgoing[:, :, pl.ds(1024, 128)] = jnp.dot(picking, row_of, preferred_element_type=F32).reshape(16, 8, 128).astype(BF)
    own = pltpu.make_async_copy(text_pairs, text_all.at[y, k], load.at[5])
    own.start()
    text_ring = Ring(at, "y", lambda coordinate, half: text_all.at[coordinate, k, pl.ds(64 * half, 64)], send, recv, 54)
    visual_ring = Ring(at, "y", lambda coordinate, half: visual_all.at[coordinate, k, pl.ds(16 * half, 16)], send, recv, 60)
    pair_forwards, copies, stored = [], [], []

    def transpose(chunk):
        if chunk >= 2:
            stored[chunk - 2].wait()

        def step(i, carry):
            lanes = pl.ds(pl.multiple_of(i * 128, 128), 128)
            block_t[chunk % 2, :, lanes] = weight[pl.ds(chunk * 8 + i, 1)].reshape(128, 1024).T
            return carry

        lax.fori_loop(0, 8, step, 0)
        copy = pltpu.make_async_copy(block_t.at[chunk % 2], weight_t.at[:, pl.ds(chunk * 1024, 1024)], store.at[chunk])
        copy.start()
        stored.append(copy)

    def pass_on(ref, number):
        copy = remote(ref, ref, forward_send.at[21 + number], forward_recv.at[21 + number], partner)
        copy.start()
        pair_forwards.append(copy)

    for by in range(1, 16):
        to = lax.rem(dp + by, 16)
        copy = remote(outgoing.at[to], landed.at[dp], dp_send.at[by - 1], dp_recv.at[by - 1], (to, ctx))
        copy.start()
        copies.append(copy)
    own.wait()
    text_ring.start()
    pass_on(text_all.at[y, k], 0)
    own = pltpu.make_async_copy(outgoing.at[dp], landed.at[dp], load.at[6])
    own.start()
    transpose(0)
    transpose(1)
    own.wait()
    for by in range(1, 16):
        source = lax.rem(dp - by + 16, 16)
        remote(landed.at[source], landed.at[source], dp_send.at[by - 1], dp_recv.at[by - 1], (source, ctx)).wait_recv()
    row = lax.broadcasted_iota(jnp.int32, (128, 128), 0)
    turn = (lax.broadcasted_iota(jnp.int32, (128, 128), 1) == (row % 16) * 8 + row // 16).astype(F32).astype(BF)
    came = landed[...].astype(F32).reshape(128, 1152).astype(BF)
    turned[...] = jnp.dot(turn, came, preferred_element_type=F32).astype(BF).reshape(8, 16, 1152)
    for by in range(1, 8):
        to = lax.rem(ctx + by, 8)
        copy = remote(turned.at[to], arrived.at[ctx], ctx_send.at[by - 1], ctx_recv.at[by - 1], (dp, to))
        copy.start()
        copies.append(copy)
    own = pltpu.make_async_copy(turned.at[ctx], arrived.at[ctx], load.at[7])
    own.start()
    first, second = text_ring.relay()
    pass_on(first, 1)
    pass_on(second, 2)
    transpose(2)
    transpose(3)
    own.wait()
    for by in range(1, 8):
        source = lax.rem(ctx - by + 8, 8)
        remote(arrived.at[source], arrived.at[source], ctx_send.at[by - 1], ctx_recv.at[by - 1], (dp, source)).wait_recv()
    rows = arrived[:, :, pl.ds(1024, 128)].astype(F32).reshape(128, 128)
    lane = lax.broadcasted_iota(jnp.int32, (128, 128), 1).astype(F32)
    contract = (((0,), (0,)), ((), ()))
    begin = jnp.min(jnp.where(rows > 0.5, rows, 1000.0), axis=0, keepdims=True)
    packing = (rows - begin == lane).astype(F32).astype(BF)
    packed = lax.dot_general(
        packing, arrived[:, :, pl.ds(0, 1024)].reshape(128, 1024), contract, preferred_element_type=F32
    )
    visual_all[y, k, :, pl.ds(0, 1024)] = packed[:32].astype(BF)
    visual_all[y, k, :, pl.ds(1024, 128)] = jnp.broadcast_to(begin, (32, 128)).astype(BF)
    visual_ring.start()
    pass_on(visual_all.at[y, k], 7)
    places = (rows == lane + 1.0).astype(F32).astype(BF)
    placing[...] = places
    marked[...] = lax.dot_general(places, jnp.ones((128, 128), BF), contract, preferred_element_type=F32)
    transpose(4)
    for number in (2, 3, 4, 5):
        pass_on(text_ring.arrived(number), number + 1)
    first, second = visual_ring.relay()
    pass_on(first, 8)
    pass_on(second, 9)
    transpose(5)
    for number in (2, 3):
        pass_on(visual_ring.arrived(number), number + 8)
    transpose(6)
    for number in (4, 5):
        pass_on(visual_ring.arrived(number), number + 8)
    transpose(7)
    for copy in pair_forwards:
        copy.wait()
    for copy in copies:
        copy.wait_send()
    text_ring.finish()
    visual_ring.finish()
    stored[6].wait()
    stored[7].wait()
    for part in rings:
        for ring in part:
            ring.finish()
    for part in forwards:
        for copy in part.values():
            copy.wait_send()
    for chunk in ORDER:
        swaps[chunk].wait_send()
    ring_sum.finish()


def first_call(patches, vit_gain, up, down, text, gain, kv, dest):
    shape = jax.ShapeDtypeStruct
    dma = pltpu.SemaphoreType.DMA
    return pl.pallas_call(
        first_kernel,
        out_shape=(
            shape((4, 2, 128, 1024), BF), shape((4, 2, 32, 1152), BF), shape((128, 128), BF), shape((128, 128), F32),
            shape((1024, 8192), BF), shape((128, 1024), BF), shape((32, 1024), BF),
            shape((32, 8192), BF), shape((160, 128), F32),
        ),
        in_specs=[ANY, VM, ANY, ANY, ANY, VM, ANY, VM],
        out_specs=(VM, VM, VM, VM, ANY, VM, VM, VM, VM),
        scratch_shapes=[
            pltpu.VMEM((64, 2, 64, 1024), BF), pltpu.VMEM((256, 5120), BF), pltpu.VMEM((5120, 384), BF),
            pltpu.VMEM((384, 8192), BF), pltpu.VMEM((128, 8192), BF), pltpu.VMEM((160, 8192), BF), pltpu.VMEM((256, 384), BF),
            pltpu.VMEM((4, 2, 32, 8192), BF), pltpu.VMEM((4, 32, 8192), BF), pltpu.VMEM((4, 32, 8192), BF),
            pltpu.VMEM((4, 32, 2048), BF), pltpu.VMEM((4, 32, 2048), BF), pltpu.VMEM((4, 32, 2048), BF),
            pltpu.VMEM((160, 1024), F32), pltpu.VMEM((256, 384), F32),
            pltpu.VMEM((16, 8, 1152), BF), pltpu.VMEM((16, 8, 1152), BF), pltpu.VMEM((8, 16, 1152), BF), pltpu.VMEM((8, 16, 1152), BF),
            pltpu.VMEM((2, 1024, 1024), BF),
            dma((8,)), dma((66,)), dma((66,)), dma((35,)), dma((35,)), dma((4,)), dma((4,)), dma((12,)), dma((12,)), dma((8,)),
            dma((7,)), dma((7,)), dma((15,)), dma((15,)),
        ],
        compiler_params=pltpu.CompilerParams(collective_id=1, has_side_effects=True, vmem_limit_bytes=VMEM_ALL),
        name="merge_and_project",
    )(patches, vit_gain, up, down, text, gain, kv, dest)


WINDOWS = (2, 3, 4, 5)


def attend_kernel(assign, own, text_all, visual_all, docs, queries, upstream, attn_out, q_grad, pair_grads, held, turned):
    head = pl.program_id(0)

    @pl.when(head == 0)
    def _():
        row = lax.broadcasted_iota(jnp.int32, (128, 32), 0)
        column = lax.broadcasted_iota(jnp.int32, (128, 32), 1)

        def fill(source, carry):
            begin = visual_all[source, 0:1, 1024:1025].astype(F32).astype(jnp.int32) - 1
            spread = (row - column == begin).astype(F32).astype(BF)
            placed = jnp.dot(spread, visual_all[source, :, 0:1024], preferred_element_type=F32)
            inside = (row[:, 0:1] >= begin) & (row[:, 0:1] < begin + 32)
            both = jnp.where(inside, placed, text_all[source].astype(F32)).astype(BF)
            held[assign[2 * source]] = both[:64]
            held[assign[2 * source + 1]] = both[64:]
            return carry

        lax.fori_loop(0, 8, fill, 0)

    labels = docs[...]
    starts = [jnp.sum((labels < d).astype(F32)).astype(jnp.int32) for d in (1, 2, 3)]
    key_columns = pl.ds(pl.multiple_of(head * HD, HD), HD)
    value_columns = pl.ds(pl.multiple_of(KVH * HD + head * HD, HD), HD)
    turned[...] = jnp.zeros_like(turned)
    score_scale = HD**-0.5
    outer = (((0,), (0,)), ((), ()))
    inner = (((1,), (1,)), ((), ()))

    def attend(half, position, chunks):
        window = chunks * 128
        low = jnp.maximum(position // 2 - (chunks - 1), 0)
        rows = pl.ds(pl.multiple_of(half * 64, 64), 64)
        query = jnp.concatenate([queries[rows, g * HD : (g + 1) * HD] for g in range(GROUP)], axis=0)
        grad = jnp.concatenate([upstream[rows, g * HD : (g + 1) * HD] for g in range(GROUP)], axis=0)
        blocks = pl.ds(low * 2, window // 64)
        keys = held[blocks, :, key_columns].reshape(window, HD)
        values = held[blocks, :, value_columns].reshape(window, HD)
        query_at = position * 64 + lax.broadcasted_iota(jnp.int32, (64, window), 0)
        key_at = low * 128 + lax.broadcasted_iota(jnp.int32, (64, window), 1)
        begin = jnp.zeros((64, window), jnp.int32)
        for start in starts:
            begin = jnp.where(query_at >= start, start, begin)
        allowed = (key_at <= query_at) & (key_at >= begin)
        scores = lax.dot_general(query, keys, inner, preferred_element_type=F32).reshape(GROUP, 64, window)
        scores = jnp.where(allowed[None], scores * (score_scale * math.log2(math.e)), -1e30)
        weights = jnp.exp2(scores - jnp.max(scores, axis=-1, keepdims=True))
        weights = weights * (1.0 / jnp.sum(weights, axis=-1, keepdims=True))
        weights = weights.reshape(GROUP * 64, window)
        light = weights.astype(BF)
        output = jnp.dot(light, values, preferred_element_type=F32)
        weight_grad = lax.dot_general(grad, values, inner, preferred_element_type=F32)
        inner_sum = jnp.sum(weights * weight_grad, axis=-1, keepdims=True)
        score_grad = (weights * (weight_grad - inner_sum)).astype(BF)
        query_grad = jnp.dot(score_grad, keys, preferred_element_type=F32) * score_scale
        window_at = pl.ds(pl.multiple_of(low * 128, 128), window)
        turned[0, :, window_at] += lax.dot_general(query, score_grad, outer, preferred_element_type=F32)
        turned[1, :, window_at] += lax.dot_general(grad, light, outer, preferred_element_type=F32)
        for g in range(GROUP):
            attn_out[rows, g * HD : (g + 1) * HD] = output[g * 64 : (g + 1) * 64].astype(BF)
            q_grad[rows, g * HD : (g + 1) * HD] = query_grad[g * 64 : (g + 1) * 64].astype(BF)

    def one_half(half, carry):
        position = assign[own[0] * 2 + half]
        begin = jnp.int32(0)
        for start in starts:
            begin = jnp.where(position * 64 >= start, start, begin)
        need = position // 2 - begin // 128 + 1
        for chunks in WINDOWS:
            fits = need <= chunks if chunks == WINDOWS[0] else need == chunks

            @pl.when(fits)
            def _(chunks=chunks):
                attend(half, position, chunks)

        return carry

    lax.fori_loop(0, 2, one_half, 0)
    held[:, :, key_columns] = (turned[0] * score_scale).T.reshape(16, 64, HD).astype(BF)
    held[:, :, value_columns] = turned[1].T.reshape(16, 64, HD).astype(BF)
    for block in range(16):
        pair_grads[block, :, key_columns] = held[assign[block], :, key_columns]
        pair_grads[block, :, value_columns] = held[assign[block], :, value_columns]


def attend_call(assign, own, text_all, visual_all, docs, queries, upstream):
    shape = jax.ShapeDtypeStruct
    by_head = pl.BlockSpec((128, GROUP * HD), lambda head, *_: (0, head))

    def whole(*dims):
        return pl.BlockSpec(dims, lambda head, *_: (0,) * len(dims))

    return pl.pallas_call(
        attend_kernel,
        out_shape=(shape((128, 4096), BF), shape((128, 4096), BF), shape((16, 64, 1024), BF)),
        grid_spec=pltpu.PrefetchScalarGridSpec(
            num_scalar_prefetch=2,
            grid=(KVH,),
            in_specs=[whole(8, 128, 1024), whole(8, 32, 1152), whole(1, 1024), by_head, by_head],
            out_specs=(by_head, by_head, whole(16, 64, 1024)),
            scratch_shapes=[pltpu.VMEM((16, 64, 1024), BF), pltpu.VMEM((2, HD, 1024), F32)],
        ),
        compiler_params=pltpu.CompilerParams(vmem_limit_bytes=VMEM_ALL),
        name="attend",
    )(assign, own, text_all, visual_all, docs, queries, upstream)


def return_kernel(
    grads, placing_hbm, dest, own_grad, visual_grad,
    kept, placing, from_partner, sums, far, plain, through, leaving, landed, turned, arrived,
    load, pair_send, pair_recv, sum_send, sum_recv, dp_send, dp_recv, ctx_send, ctx_recv,
):
    at = place()
    dp, ctx = lax.axis_index("dp"), lax.axis_index("ctx")
    k, y = at["k"], at["y"]
    own = [
        pltpu.make_async_copy(grads.at[:, k], kept, load.at[2]),
        pltpu.make_async_copy(placing_hbm, placing, load.at[3]),
    ]
    for copy in own:
        copy.start()
    greet([(dp, lax.rem(ctx + by, 8)) for by in range(1, 8)] + [(lax.rem(dp + by, 16), ctx) for by in range(1, 16)])
    partner = device(shifted(at, "k", 1))
    width = 256
    swaps = {}
    for chunk in ORDER:
        columns = pl.ds(chunk * width, width)
        swaps[chunk] = remote(
            grads.at[:, 1 - k, :, columns], from_partner.at[:, :, columns], pair_send.at[chunk], pair_recv.at[chunk], partner
        )
        swaps[chunk].start()
    ring_sum = RingSum(at, sums, far, plain, through, 4, sum_send, sum_recv)
    for copy in own:
        copy.wait()
    for chunk in ORDER:
        swaps[chunk].wait_recv()
        columns = pl.ds(chunk * width, width)
        for block in range(4):
            mine = kept[block, :, columns]
            sums[block, :, columns] = (mine.astype(F32) + from_partner[block, :, columns].astype(F32)).astype(BF)
        ring_sum.start(chunk)
    for chunk in ORDER:
        ring_sum.relay(chunk)
    for chunk in ORDER:
        own_grad[:, pl.ds(chunk * width, width)] = ring_sum.total(chunk).astype(BF)
    leaving[...] = jnp.dot(placing[...], own_grad[...], preferred_element_type=F32).astype(BF).reshape(8, 16, 1024)
    own = pltpu.make_async_copy(leaving.at[ctx], landed.at[ctx], load.at[0])
    own.start()
    copies = []
    for by in range(1, 8):
        to = lax.rem(ctx + by, 8)
        copy = remote(leaving.at[to], landed.at[ctx], ctx_send.at[by - 1], ctx_recv.at[by - 1], (dp, to))
        copy.start()
        copies.append(copy)
    own.wait()
    for by in range(1, 8):
        source = lax.rem(ctx - by + 8, 8)
        remote(landed.at[source], landed.at[source], ctx_send.at[by - 1], ctx_recv.at[by - 1], (dp, source)).wait_recv()
    row = lax.broadcasted_iota(jnp.int32, (128, 128), 0)
    turn = (lax.broadcasted_iota(jnp.int32, (128, 128), 1) == (row % 8) * 16 + row // 8).astype(F32).astype(BF)
    turned[...] = jnp.dot(turn, landed[...].reshape(128, 1024), preferred_element_type=F32).reshape(16, 8, 1024).astype(BF)
    for by in range(1, 16):
        to = lax.rem(dp + by, 16)
        copy = remote(turned.at[to], arrived.at[dp], dp_send.at[by - 1], dp_recv.at[by - 1], (to, ctx))
        copy.start()
        copies.append(copy)
    own = pltpu.make_async_copy(turned.at[dp], arrived.at[dp], load.at[1])
    own.start()
    own.wait()
    for by in range(1, 16):
        source = lax.rem(dp - by + 16, 16)
        remote(arrived.at[source], arrived.at[source], dp_send.at[by - 1], dp_recv.at[by - 1], (source, ctx)).wait_recv()
    target = jnp.broadcast_to(upright(dest[...].reshape(1, 32) // 128), (32, 128))
    picking = (target == lax.broadcasted_iota(jnp.int32, (32, 128), 1).astype(F32)).astype(F32).astype(BF)
    came = arrived[...].astype(F32).reshape(128, 1024).astype(BF)
    visual_grad[...] = jnp.dot(picking, came, preferred_element_type=F32).astype(BF)
    for copy in copies:
        copy.wait_send()
    for chunk in ORDER:
        swaps[chunk].wait_send()
    ring_sum.finish()


def return_call(grads, placing, dest):
    shape = jax.ShapeDtypeStruct
    dma = pltpu.SemaphoreType.DMA
    return pl.pallas_call(
        return_kernel,
        out_shape=(shape((128, 1024), BF), shape((32, 1024), BF)),
        in_specs=[ANY, ANY, VM],
        out_specs=(VM, VM),
        scratch_shapes=[
            pltpu.VMEM((4, 128, 1024), BF), pltpu.VMEM((128, 128), BF),
            pltpu.VMEM((4, 128, 1024), BF), pltpu.VMEM((4, 128, 1024), BF),
            pltpu.VMEM((4, 128, 256), BF), pltpu.VMEM((4, 128, 256), BF), pltpu.VMEM((4, 128, 256), BF),
            pltpu.VMEM((8, 16, 1024), BF), pltpu.VMEM((8, 16, 1024), BF), pltpu.VMEM((16, 8, 1024), BF), pltpu.VMEM((16, 8, 1024), BF),
            dma((4,)), dma((4,)), dma((4,)), dma((12,)), dma((12,)), dma((15,)), dma((15,)), dma((7,)), dma((7,)),
        ],
        compiler_params=pltpu.CompilerParams(collective_id=3, has_side_effects=True, vmem_limit_bytes=VMEM_ALL),
        name="return_grads",
    )(grads, placing, dest)


def final_kernel(
    own_grad, visual_pair_grad, text_pairs, visual_pairs, weight, text, visual, gain, scales, marked, hidden_grad, visual_grad
):
    block = weight[...]
    gains = gain[...]

    def through(grad, pair, value, scale):
        mean = jnp.sum(grad.astype(F32) * pair.astype(F32), axis=-1, keepdims=True) * (1.0 / 8192.0)
        normed_grad = jnp.dot(grad, block, preferred_element_type=F32)
        return scale * (gains * normed_grad) - value.astype(F32) * (scale * scale * mean)

    full = through(own_grad[...], text_pairs[...], text[...], scales[0:128, 0:1])
    hidden_grad[...] = jnp.where(marked[:, 0:1] > 0.5, 0.0, full).astype(BF)
    visual_grad[...] = through(visual_pair_grad[...], visual_pairs[...], visual[...], scales[128:160, 0:1]).astype(BF)


def final_call(own_grad, visual_pair_grad, text_pairs, visual_pairs, weight, text, visual, gain, scales, marked):
    shape = jax.ShapeDtypeStruct
    tile = 1024

    def whole(*dims):
        return pl.BlockSpec(dims, lambda i: (0,) * len(dims))

    return pl.pallas_call(
        final_kernel,
        out_shape=(shape((128, 8192), BF), shape((32, 8192), BF)),
        grid=(8192 // tile,),
        in_specs=[
            whole(128, 1024), whole(32, 1024), whole(128, 1024), whole(32, 1024),
            pl.BlockSpec((1024, tile), lambda i: (0, i)), pl.BlockSpec((128, tile), lambda i: (0, i)),
            pl.BlockSpec((32, tile), lambda i: (0, i)), pl.BlockSpec((1, tile), lambda i: (0, i)),
            whole(160, 128), whole(128, 128),
        ],
        out_specs=(pl.BlockSpec((128, tile), lambda i: (0, i)), pl.BlockSpec((32, tile), lambda i: (0, i))),
        compiler_params=pltpu.CompilerParams(vmem_limit_bytes=VMEM_ALL),
        name="through_norm",
    )(own_grad, visual_pair_grad, text_pairs, visual_pairs, weight, text, visual, gain, scales, marked)


def local(patches, vit_gain, merge_up, merge_down, dest, text, norm_gain, kv_weight, queries, out_grad, assign, docs):
    gain = norm_gain.reshape(1, 8192)
    text_all, visual_all, placing, marked, weight_t, text_pairs, visual_pairs, visual, scales = first_call(
        patches, vit_gain, merge_up, merge_down, text[0], gain, kv_weight, dest
    )
    own = lax.axis_index("ctx").astype(jnp.int32).reshape(1)
    attention, query_grad, pair_grads = attend_call(
        assign, own, text_all.reshape(8, 128, 1024), visual_all.reshape(8, 32, 1152), docs, queries[0], out_grad[0]
    )
    own_grad, visual_pair_grad = return_call(pair_grads.reshape(4, 2, 128, 1024), placing, dest)
    hidden_grad, visual_grad = final_call(
        own_grad, visual_pair_grad, text_pairs, visual_pairs, weight_t, text[0], visual, gain, scales, marked
    )
    return attention[None], query_grad[None], hidden_grad[None], visual_grad


def solution(mesh):
    placed = (
        P("dp", None),
        P(),
        P(None, "ctx"),
        P("ctx", None),
        P(("dp", "ctx")),
        P("dp", "ctx", None),
        P(),
        P(("dp", "ctx"), None),
        P("dp", "ctx", None),
        P("dp", "ctx", None),
        P(),
        P("dp", None),
    )
    return jax.shard_map(
        local,
        mesh=mesh,
        in_specs=placed,
        out_specs=(P("dp", "ctx", None), P("dp", "ctx", None), P("dp", "ctx", None), P(("dp", "ctx"), None)),
        check_vma=False,
    )
```

```python
import functools
import math

import jax
import jax.numpy as jnp
from jax import lax
from jax.experimental import pallas as pl
from jax.experimental.pallas import tpu as pltpu
from jax.sharding import PartitionSpec as P

MESH = pl.DeviceIdType.MESH
BF = jnp.bfloat16
F32 = jnp.float32
HEADS = 32
KVH = 4
HD = 128
GROUP = HEADS // KVH
EPS = 1e-06
VMEM_ALL = 67043328
ANY = pl.BlockSpec(memory_space=pl.ANY)
VM = pl.BlockSpec(memory_space=pltpu.VMEM)


def place():
    dp, ctx = lax.axis_index("dp"), lax.axis_index("ctx")
    return {"x": dp // 4, "z": dp % 4, "y": ctx // 2, "k": ctx % 2}


def device(at):
    return (at["x"] * 4 + at["z"], at["y"] * 2 + at["k"])


def shifted(at, axis, by):
    size = 2 if axis == "k" else 4
    return dict(at, **{axis: lax.rem(at[axis] + by + size, size)})


def remote(src, dst, send, recv, to):
    return pltpu.make_async_remote_copy(
        src_ref=src, dst_ref=dst, send_sem=send, recv_sem=recv, device_id=to, device_id_type=MESH
    )


def greet(devices):
    barrier = pltpu.get_barrier_semaphore()
    for to in devices:
        pl.semaphore_signal(barrier, inc=1, device_id=to, device_id_type=MESH)
    pl.semaphore_wait(barrier, len(devices))


def upright(row):
    same = lax.broadcasted_iota(jnp.int32, (32, 32), 0) == lax.broadcasted_iota(jnp.int32, (32, 32), 1)
    return jnp.sum(jnp.where(same, jnp.broadcast_to(row, (32, 32)), 0).astype(F32), axis=1, keepdims=True)


class Ring:
    def __init__(self, at, axis, slab, send, recv, base):
        self.at, self.axis, self.slab, self.send, self.recv, self.base = at, axis, slab, send, recv, base
        self.plus, self.minus = device(shifted(at, axis, 1)), device(shifted(at, axis, -1))
        self.sent = []

    def _coordinate(self, by):
        return shifted(self.at, self.axis, by)[self.axis]

    def _copy(self, by, half, number, to):
        ref = self.slab(self._coordinate(by), half)
        copy = remote(ref, ref, self.send.at[self.base + number], self.recv.at[self.base + number], to)
        copy.start()
        self.sent.append(copy)

    def start(self):
        self._copy(0, 0, 0, self.plus)
        self._copy(0, 1, 1, self.minus)
        self._copy(0, 1, 2, self.plus)
        self._copy(0, 0, 3, self.minus)

    ARRIVALS = ((-1, 0), (1, 1), (-1, 1), (1, 0), (2, 0), (2, 1))

    def arrived(self, number):
        by, half = self.ARRIVALS[number]
        ref = self.slab(self._coordinate(by), half)
        remote(ref, ref, self.send.at[self.base + number], self.recv.at[self.base + number], self.plus).wait_recv()
        return ref

    def relay(self):
        first, second = self.arrived(0), self.arrived(1)
        self._copy(-1, 0, 4, self.plus)
        self._copy(1, 1, 5, self.minus)
        return first, second

    def finish(self):
        for copy in self.sent:
            copy.wait_send()


class RingSum:
    def __init__(self, at, sums, far, plain, through, chunks, send, recv):
        self.at, self.sums, self.far, self.plain, self.through = at, sums, far, plain, through
        self.chunks, self.send, self.recv = chunks, send, recv
        self.width = sums.shape[2] // chunks
        self.sent = []

    def _block(self, by, chunk):
        y = shifted(self.at, "y", by)["y"]
        return self.sums.at[y, :, pl.ds(chunk * self.width, self.width)]

    def _way(self, chunk):
        return 1 if chunk < self.chunks // 2 else -1

    def _copy(self, src, dst, number, by):
        copy = remote(src, dst, self.send.at[number], self.recv.at[number], device(shifted(self.at, "y", by)))
        copy.start()
        self.sent.append(copy)

    def _wait(self, dst, number):
        remote(dst, dst, self.send.at[number], self.recv.at[number], device(shifted(self.at, "y", 1))).wait_recv()

    def start(self, chunk):
        way = self._way(chunk)
        self._copy(self._block(2, chunk), self.far.at[chunk], chunk * 3, way)
        self._copy(self._block(-way, chunk), self.plain.at[chunk], chunk * 3 + 1, -way)

    def relay(self, chunk):
        way = self._way(chunk)
        self._wait(self.far.at[chunk], chunk * 3)
        block = self._block(way, chunk)
        block[...] = (block[...].astype(F32) + self.far[chunk].astype(F32)).astype(BF)
        self._copy(block, self.through.at[chunk], chunk * 3 + 2, way)

    def total(self, chunk):
        self._wait(self.plain.at[chunk], chunk * 3 + 1)
        self._wait(self.through.at[chunk], chunk * 3 + 2)
        own = self._block(0, chunk)[...].astype(F32)
        return own + self.plain[chunk].astype(F32) + self.through[chunk].astype(F32)

    def finish(self):
        for copy in self.sent:
            copy.wait_send()


PARTS = ((0, 384, "yzx"), (384, 384, "xyz"), (768, 256, "zxy"))
STEPS = (0, -1, 1, 2)
ORDER = (0, 2, 1, 3)


def first_kernel(
    patches_hbm, vit_gain, up_hbm, down_hbm, text_hbm, gain, kv_hbm, dest,
    text_all, visual_all, placing, marked, weight_t, text_pairs, visual_pairs, visual_out, scales,
    weight, patches, up, down, text, normed, hidden, partial, from_partner, sums, far, plain, through, acc, inner,
    outgoing, landed, turned, arrived, block_t,
    load, send, recv, forward_send, forward_recv, pair_send, pair_recv, sum_send, sum_recv, store,
    ctx_send, ctx_recv, dp_send, dp_recv,
):
    at = place()
    k, y = at["k"], at["y"]
    chip = (at["x"] * 4 + at["z"]) * 4 + y
    own = pltpu.make_async_copy(kv_hbm, weight.at[chip, k], load.at[0])
    own.start()
    loads = []
    for number, (src, dst) in enumerate(((patches_hbm, patches), (up_hbm, up), (down_hbm, down), (text_hbm, text))):
        copy = pltpu.make_async_copy(src, dst, load.at[number + 1])
        copy.start()
        loads.append(copy)
    partner = device(shifted(at, "k", 1))
    dp, ctx = lax.axis_index("dp"), lax.axis_index("ctx")
    greet([(dp, lax.rem(ctx + by, 8)) for by in range(1, 8)] + [(lax.rem(dp + by, 16), ctx) for by in range(1, 16)])
    own.wait()

    def slab_of(axes_done, axis, first, count):
        def slab(coordinate, half):
            cut = {name: (pl.ds(0, 4) if name in axes_done else pl.ds(at[name], 1)) for name in "xyz"}
            cut[axis] = pl.ds(coordinate, 1)
            return weight6.at[cut["x"], cut["z"], cut["y"], k, pl.ds(32 * half, 32), pl.ds(first, count)]

        return slab

    weight6 = weight.reshape(4, 4, 4, 2, 64, 1024)
    rings = [
        [
            Ring(at, order[phase], slab_of(order[:phase], order[phase], first, count), send, recv, (part * 3 + phase) * 6)
            for phase in range(3)
        ]
        for part, (first, count, order) in enumerate(PARTS)
    ]
    forwards = [{} for _ in PARTS]

    def forward(ref, number):
        copy = remote(ref, ref, forward_send.at[number], forward_recv.at[number], partner)
        copy.start()
        forwards[number // 7][number % 7] = copy

    for part in rings:
        part[0].start()

    loads[0].wait()
    vg = vit_gain[...].reshape(1, 1280)

    def norm_rows(step, carry):
        rows = pl.ds(pl.multiple_of(step * 16, 16), 16)
        for piece in range(4):
            columns = pl.ds(piece * 1280, 1280)
            value = patches[rows, columns].astype(F32)
            center = value - jnp.mean(value, axis=-1, keepdims=True)
            spread = jnp.mean(center * center, axis=-1, keepdims=True)
            patches[rows, columns] = (center * lax.rsqrt(spread + EPS) * vg).astype(BF)
        return carry

    lax.fori_loop(0, 6, norm_rows, 0)
    for part in rings:
        part[0].relay()
    lax.fori_loop(6, 16, norm_rows, 0)
    for part in rings:
        for number in (2, 3, 4, 5):
            part[0].arrived(number)
        part[1].start()
    loads[1].wait()
    inner[...] = jnp.zeros_like(inner)

    def up_step(step, carry):
        columns = pl.ds(pl.multiple_of(step * 1024, 1024), 1024)
        inner[...] += jnp.dot(patches[:, columns], up[columns, :], preferred_element_type=F32)
        return carry

    lax.fori_loop(0, 5, up_step, 0)
    value = inner[...]
    hidden[...] = (0.5 * value * (1.0 + lax.erf(value * (1.0 / math.sqrt(2.0))))).astype(BF)
    loads[2].wait()

    width = 2048
    swaps = {}
    for chunk in ORDER:
        def down_step(step, carry, chunk=chunk):
            columns = pl.ds(pl.multiple_of(chunk * width + step * 512, 512), 512)
            product = jnp.dot(hidden[...], down[:, columns], preferred_element_type=F32)
            partial[:, :, :, columns] = product.astype(BF).reshape(4, 2, 32, 512)
            return carry

        lax.fori_loop(0, 4, down_step, 0)
        columns = pl.ds(chunk * width, width)
        swaps[chunk] = remote(
            partial.at[:, 1 - k, :, columns], from_partner.at[:, :, columns], pair_send.at[chunk], pair_recv.at[chunk], partner
        )
        swaps[chunk].start()
        if chunk == 2:
            for part in rings:
                part[1].relay()
    ring_sum = RingSum(at, sums, far, plain, through, 4, sum_send, sum_recv)
    for chunk in ORDER:
        swaps[chunk].wait_recv()
        columns = pl.ds(chunk * width, width)
        for block in range(4):
            mine = partial[block, pl.ds(k, 1), :, columns].reshape(32, width)
            sums[block, :, columns] = (mine.astype(F32) + from_partner[block, :, columns].astype(F32)).astype(BF)
        ring_sum.start(chunk)
    for number, part in enumerate(rings):
        for arrival in (2, 3, 4, 5):
            part[1].arrived(arrival)
        part[2].start()
        order = PARTS[number][2]
        cut = {name: (pl.ds(at[name], 1) if name == order[2] else pl.ds(0, 4)) for name in "xyz"}
        forward(weight6.at[cut["x"], cut["z"], cut["y"], k, :, pl.ds(PARTS[number][0], PARTS[number][1])], number * 7)

    loads[3].wait()

    def text_rows(step, carry):
        rows = pl.ds(pl.multiple_of(step * 16, 16), 16)
        value = text[rows, :].astype(F32)
        scale = lax.rsqrt(jnp.mean(value * value, axis=-1, keepdims=True) + EPS)
        normed[rows, :] = (value * scale * gain[...]).astype(BF)
        scales[rows, :] = jnp.broadcast_to(scale, (16, 128))
        return carry

    lax.fori_loop(0, 8, text_rows, 0)
    for chunk in ORDER:
        ring_sum.relay(chunk)
    for number, part in enumerate(rings):
        first, second = part[2].relay()
        forward(first, number * 7 + 1)
        forward(second, number * 7 + 2)
    for number, part in enumerate(rings):
        for arrival in (2, 3):
            forward(part[2].arrived(arrival), number * 7 + 1 + arrival)
    for chunk in ORDER:
        visual_out[:, pl.ds(chunk * width, width)] = ring_sum.total(chunk).astype(BF)
    for step in range(2):
        rows = pl.ds(step * 16, 16)
        value = visual_out[rows, :].astype(F32)
        scale = lax.rsqrt(jnp.mean(value * value, axis=-1, keepdims=True) + EPS)
        normed[pl.ds(128 + step * 16, 16), :] = (value * scale * gain[...]).astype(BF)
        scales[pl.ds(128 + step * 16, 16), :] = jnp.broadcast_to(scale, (16, 128))
    for number, part in enumerate(rings):
        for arrival in (4, 5):
            forward(part[2].arrived(arrival), number * 7 + 1 + arrival)
    for part in forwards:
        for copy in part.values():
            copy.wait_recv()
    acc[...] = jnp.zeros_like(acc)

    def project(step, carry):
        columns = pl.ds(pl.multiple_of(step * 2048, 2048), 2048)
        block = weight[pl.ds(step * 16, 16)].reshape(2048, 1024)
        acc[...] += jnp.dot(normed[:, columns], block, preferred_element_type=F32)
        return carry

    lax.fori_loop(0, 4, project, 0)
    text_pairs[...] = acc[pl.ds(0, 128), :].astype(BF)
    mine = acc[pl.ds(128, 32), :].astype(BF)
    visual_pairs[...] = mine
    entry = dest[...].reshape(1, 32)
    row_of = jnp.broadcast_to(upright(entry % 128 + 1), (32, 128)).astype(BF)
    picking = (lax.broadcasted_iota(jnp.int32, (128, 32), 0) == entry // 128).astype(F32).astype(BF)
    outgoing[:, :, pl.ds(0, 1024)] = jnp.dot(picking, mine, preferred_element_type=F32).reshape(16, 8, 1024).astype(BF)
    outgoing[:, :, pl.ds(1024, 128)] = jnp.dot(picking, row_of, preferred_element_type=F32).reshape(16, 8, 128).astype(BF)
    own = pltpu.make_async_copy(text_pairs, text_all.at[y, k], load.at[5])
    own.start()
    text_ring = Ring(at, "y", lambda coordinate, half: text_all.at[coordinate, k, pl.ds(64 * half, 64)], send, recv, 54)
    visual_ring = Ring(at, "y", lambda coordinate, half: visual_all.at[coordinate, k, pl.ds(16 * half, 16)], send, recv, 60)
    pair_forwards, copies, stored = [], [], []

    def transpose(chunk):
        if chunk >= 2:
            stored[chunk - 2].wait()

        def step(i, carry):
            lanes = pl.ds(pl.multiple_of(i * 128, 128), 128)
            block_t[chunk % 2, :, lanes] = weight[pl.ds(chunk * 8 + i, 1)].reshape(128, 1024).T
            return carry

        lax.fori_loop(0, 8, step, 0)
        copy = pltpu.make_async_copy(block_t.at[chunk % 2], weight_t.at[:, pl.ds(chunk * 1024, 1024)], store.at[chunk])
        copy.start()
        stored.append(copy)

    def pass_on(ref, number):
        copy = remote(ref, ref, forward_send.at[21 + number], forward_recv.at[21 + number], partner)
        copy.start()
        pair_forwards.append(copy)

    for by in range(1, 16):
        to = lax.rem(dp + by, 16)
        copy = remote(outgoing.at[to], landed.at[dp], dp_send.at[by - 1], dp_recv.at[by - 1], (to, ctx))
        copy.start()
        copies.append(copy)
    own.wait()
    text_ring.start()
    pass_on(text_all.at[y, k], 0)
    own = pltpu.make_async_copy(outgoing.at[dp], landed.at[dp], load.at[6])
    own.start()
    transpose(0)
    transpose(1)
    own.wait()
    for by in range(1, 16):
        source = lax.rem(dp - by + 16, 16)
        remote(landed.at[source], landed.at[source], dp_send.at[by - 1], dp_recv.at[by - 1], (source, ctx)).wait_recv()
    row = lax.broadcasted_iota(jnp.int32, (128, 128), 0)
    turn = (lax.broadcasted_iota(jnp.int32, (128, 128), 1) == (row % 16) * 8 + row // 16).astype(F32).astype(BF)
    came = landed[...].astype(F32).reshape(128, 1152).astype(BF)
    turned[...] = jnp.dot(turn, came, preferred_element_type=F32).astype(BF).reshape(8, 16, 1152)
    for by in range(1, 8):
        to = lax.rem(ctx + by, 8)
        copy = remote(turned.at[to], arrived.at[ctx], ctx_send.at[by - 1], ctx_recv.at[by - 1], (dp, to))
        copy.start()
        copies.append(copy)
    own = pltpu.make_async_copy(turned.at[ctx], arrived.at[ctx], load.at[7])
    own.start()
    first, second = text_ring.relay()
    pass_on(first, 1)
    pass_on(second, 2)
    transpose(2)
    transpose(3)
    own.wait()
    for by in range(1, 8):
        source = lax.rem(ctx - by + 8, 8)
        remote(arrived.at[source], arrived.at[source], ctx_send.at[by - 1], ctx_recv.at[by - 1], (dp, source)).wait_recv()
    rows = arrived[:, :, pl.ds(1024, 128)].astype(F32).reshape(128, 128)
    lane = lax.broadcasted_iota(jnp.int32, (128, 128), 1).astype(F32)
    contract = (((0,), (0,)), ((), ()))
    begin = jnp.min(jnp.where(rows > 0.5, rows, 1000.0), axis=0, keepdims=True)
    packing = (rows - begin == lane).astype(F32).astype(BF)
    packed = lax.dot_general(
        packing, arrived[:, :, pl.ds(0, 1024)].reshape(128, 1024), contract, preferred_element_type=F32
    )
    visual_all[y, k, :, pl.ds(0, 1024)] = packed[:32].astype(BF)
    visual_all[y, k, :, pl.ds(1024, 128)] = jnp.broadcast_to(begin, (32, 128)).astype(BF)
    visual_ring.start()
    pass_on(visual_all.at[y, k], 7)
    places = (rows == lane + 1.0).astype(F32).astype(BF)
    placing[...] = places
    marked[...] = lax.dot_general(places, jnp.ones((128, 128), BF), contract, preferred_element_type=F32)
    transpose(4)
    for number in (2, 3, 4, 5):
        pass_on(text_ring.arrived(number), number + 1)
    first, second = visual_ring.relay()
    pass_on(first, 8)
    pass_on(second, 9)
    transpose(5)
    for number in (2, 3):
        pass_on(visual_ring.arrived(number), number + 8)
    transpose(6)
    for number in (4, 5):
        pass_on(visual_ring.arrived(number), number + 8)
    transpose(7)
    for copy in pair_forwards:
        copy.wait()
    for copy in copies:
        copy.wait_send()
    text_ring.finish()
    visual_ring.finish()
    stored[6].wait()
    stored[7].wait()
    for part in rings:
        for ring in part:
            ring.finish()
    for part in forwards:
        for copy in part.values():
            copy.wait_send()
    for chunk in ORDER:
        swaps[chunk].wait_send()
    ring_sum.finish()


def first_call(patches, vit_gain, up, down, text, gain, kv, dest):
    shape = jax.ShapeDtypeStruct
    dma = pltpu.SemaphoreType.DMA
    return pl.pallas_call(
        first_kernel,
        out_shape=(
            shape((4, 2, 128, 1024), BF), shape((4, 2, 32, 1152), BF), shape((128, 128), BF), shape((128, 128), F32),
            shape((1024, 8192), BF), shape((128, 1024), BF), shape((32, 1024), BF),
            shape((32, 8192), BF), shape((160, 128), F32),
        ),
        in_specs=[ANY, VM, ANY, ANY, ANY, VM, ANY, VM],
        out_specs=(VM, VM, VM, VM, ANY, VM, VM, VM, VM),
        scratch_shapes=[
            pltpu.VMEM((64, 2, 64, 1024), BF), pltpu.VMEM((256, 5120), BF), pltpu.VMEM((5120, 384), BF),
            pltpu.VMEM((384, 8192), BF), pltpu.VMEM((128, 8192), BF), pltpu.VMEM((160, 8192), BF), pltpu.VMEM((256, 384), BF),
            pltpu.VMEM((4, 2, 32, 8192), BF), pltpu.VMEM((4, 32, 8192), BF), pltpu.VMEM((4, 32, 8192), BF),
            pltpu.VMEM((4, 32, 2048), BF), pltpu.VMEM((4, 32, 2048), BF), pltpu.VMEM((4, 32, 2048), BF),
            pltpu.VMEM((160, 1024), F32), pltpu.VMEM((256, 384), F32),
            pltpu.VMEM((16, 8, 1152), BF), pltpu.VMEM((16, 8, 1152), BF), pltpu.VMEM((8, 16, 1152), BF), pltpu.VMEM((8, 16, 1152), BF),
            pltpu.VMEM((2, 1024, 1024), BF),
            dma((8,)), dma((66,)), dma((66,)), dma((35,)), dma((35,)), dma((4,)), dma((4,)), dma((12,)), dma((12,)), dma((8,)),
            dma((7,)), dma((7,)), dma((15,)), dma((15,)),
        ],
        compiler_params=pltpu.CompilerParams(collective_id=1, has_side_effects=True, vmem_limit_bytes=VMEM_ALL),
        name="merge_and_project",
    )(patches, vit_gain, up, down, text, gain, kv, dest)


WINDOWS = (2, 3, 4, 5)


def attend_kernel(assign, own, text_all, visual_all, docs, queries, upstream, attn_out, q_grad, pair_grads, held, turned):
    head = pl.program_id(0)

    @pl.when(head == 0)
    def _():
        row = lax.broadcasted_iota(jnp.int32, (128, 32), 0)
        column = lax.broadcasted_iota(jnp.int32, (128, 32), 1)

        def fill(source, carry):
            begin = visual_all[source, 0:1, 1024:1025].astype(F32).astype(jnp.int32) - 1
            spread = (row - column == begin).astype(F32).astype(BF)
            placed = jnp.dot(spread, visual_all[source, :, 0:1024], preferred_element_type=F32)
            inside = (row[:, 0:1] >= begin) & (row[:, 0:1] < begin + 32)
            both = jnp.where(inside, placed, text_all[source].astype(F32)).astype(BF)
            held[assign[2 * source]] = both[:64]
            held[assign[2 * source + 1]] = both[64:]
            return carry

        lax.fori_loop(0, 8, fill, 0)

    labels = docs[...]
    starts = [jnp.sum((labels < d).astype(F32)).astype(jnp.int32) for d in (1, 2, 3)]
    key_columns = pl.ds(pl.multiple_of(head * HD, HD), HD)
    value_columns = pl.ds(pl.multiple_of(KVH * HD + head * HD, HD), HD)
    turned[...] = jnp.zeros_like(turned)
    score_scale = HD**-0.5
    outer = (((0,), (0,)), ((), ()))
    inner = (((1,), (1,)), ((), ()))

    def attend(half, position, chunks):
        window = chunks * 128
        low = jnp.maximum(position // 2 - (chunks - 1), 0)
        rows = pl.ds(pl.multiple_of(half * 64, 64), 64)
        query = jnp.concatenate([queries[rows, g * HD : (g + 1) * HD] for g in range(GROUP)], axis=0)
        grad = jnp.concatenate([upstream[rows, g * HD : (g + 1) * HD] for g in range(GROUP)], axis=0)
        blocks = pl.ds(low * 2, window // 64)
        keys = held[blocks, :, key_columns].reshape(window, HD)
        values = held[blocks, :, value_columns].reshape(window, HD)
        query_at = position * 64 + lax.broadcasted_iota(jnp.int32, (64, window), 0)
        key_at = low * 128 + lax.broadcasted_iota(jnp.int32, (64, window), 1)
        begin = jnp.zeros((64, window), jnp.int32)
        for start in starts:
            begin = jnp.where(query_at >= start, start, begin)
        allowed = (key_at <= query_at) & (key_at >= begin)
        scores = lax.dot_general(query, keys, inner, preferred_element_type=F32).reshape(GROUP, 64, window)
        scores = jnp.where(allowed[None], scores * (score_scale * math.log2(math.e)), -1e30)
        weights = jnp.exp2(scores - jnp.max(scores, axis=-1, keepdims=True))
        weights = weights * (1.0 / jnp.sum(weights, axis=-1, keepdims=True))
        weights = weights.reshape(GROUP * 64, window)
        light = weights.astype(BF)
        output = jnp.dot(light, values, preferred_element_type=F32)
        weight_grad = lax.dot_general(grad, values, inner, preferred_element_type=F32)
        inner_sum = jnp.sum(weights * weight_grad, axis=-1, keepdims=True)
        score_grad = (weights * (weight_grad - inner_sum)).astype(BF)
        query_grad = jnp.dot(score_grad, keys, preferred_element_type=F32) * score_scale
        window_at = pl.ds(pl.multiple_of(low * 128, 128), window)
        turned[0, :, window_at] += lax.dot_general(query, score_grad, outer, preferred_element_type=F32)
        turned[1, :, window_at] += lax.dot_general(grad, light, outer, preferred_element_type=F32)
        for g in range(GROUP):
            attn_out[rows, g * HD : (g + 1) * HD] = output[g * 64 : (g + 1) * 64].astype(BF)
            q_grad[rows, g * HD : (g + 1) * HD] = query_grad[g * 64 : (g + 1) * 64].astype(BF)

    def one_half(half, carry):
        position = assign[own[0] * 2 + half]
        begin = jnp.int32(0)
        for start in starts:
            begin = jnp.where(position * 64 >= start, start, begin)
        need = position // 2 - begin // 128 + 1
        for chunks in WINDOWS:
            fits = need <= chunks if chunks == WINDOWS[0] else need == chunks

            @pl.when(fits)
            def _(chunks=chunks):
                attend(half, position, chunks)

        return carry

    lax.fori_loop(0, 2, one_half, 0)
    held[:, :, key_columns] = (turned[0] * score_scale).T.reshape(16, 64, HD).astype(BF)
    held[:, :, value_columns] = turned[1].T.reshape(16, 64, HD).astype(BF)
    for block in range(16):
        pair_grads[block, :, key_columns] = held[assign[block], :, key_columns]
        pair_grads[block, :, value_columns] = held[assign[block], :, value_columns]


def attend_call(assign, own, text_all, visual_all, docs, queries, upstream):
    shape = jax.ShapeDtypeStruct
    by_head = pl.BlockSpec((128, GROUP * HD), lambda head, *_: (0, head))

    def whole(*dims):
        return pl.BlockSpec(dims, lambda head, *_: (0,) * len(dims))

    return pl.pallas_call(
        attend_kernel,
        out_shape=(shape((128, 4096), BF), shape((128, 4096), BF), shape((16, 64, 1024), BF)),
        grid_spec=pltpu.PrefetchScalarGridSpec(
            num_scalar_prefetch=2,
            grid=(KVH,),
            in_specs=[whole(8, 128, 1024), whole(8, 32, 1152), whole(1, 1024), by_head, by_head],
            out_specs=(by_head, by_head, whole(16, 64, 1024)),
            scratch_shapes=[pltpu.VMEM((16, 64, 1024), BF), pltpu.VMEM((2, HD, 1024), F32)],
        ),
        compiler_params=pltpu.CompilerParams(vmem_limit_bytes=VMEM_ALL),
        name="attend",
    )(assign, own, text_all, visual_all, docs, queries, upstream)


def return_kernel(
    grads, placing_hbm, dest, own_grad, visual_grad,
    kept, placing, from_partner, sums, far, plain, through, leaving, landed, turned, arrived,
    load, pair_send, pair_recv, sum_send, sum_recv, dp_send, dp_recv, ctx_send, ctx_recv,
):
    at = place()
    dp, ctx = lax.axis_index("dp"), lax.axis_index("ctx")
    k, y = at["k"], at["y"]
    own = [
        pltpu.make_async_copy(grads.at[:, k], kept, load.at[2]),
        pltpu.make_async_copy(placing_hbm, placing, load.at[3]),
    ]
    for copy in own:
        copy.start()
    greet([(dp, lax.rem(ctx + by, 8)) for by in range(1, 8)] + [(lax.rem(dp + by, 16), ctx) for by in range(1, 16)])
    partner = device(shifted(at, "k", 1))
    width = 256
    swaps = {}
    for chunk in ORDER:
        columns = pl.ds(chunk * width, width)
        swaps[chunk] = remote(
            grads.at[:, 1 - k, :, columns], from_partner.at[:, :, columns], pair_send.at[chunk], pair_recv.at[chunk], partner
        )
        swaps[chunk].start()
    ring_sum = RingSum(at, sums, far, plain, through, 4, sum_send, sum_recv)
    for copy in own:
        copy.wait()
    for chunk in ORDER:
        swaps[chunk].wait_recv()
        columns = pl.ds(chunk * width, width)
        for block in range(4):
            mine = kept[block, :, columns]
            sums[block, :, columns] = (mine.astype(F32) + from_partner[block, :, columns].astype(F32)).astype(BF)
        ring_sum.start(chunk)
    for chunk in ORDER:
        ring_sum.relay(chunk)
    for chunk in ORDER:
        own_grad[:, pl.ds(chunk * width, width)] = ring_sum.total(chunk).astype(BF)
    leaving[...] = jnp.dot(placing[...], own_grad[...], preferred_element_type=F32).astype(BF).reshape(8, 16, 1024)
    own = pltpu.make_async_copy(leaving.at[ctx], landed.at[ctx], load.at[0])
    own.start()
    copies = []
    for by in range(1, 8):
        to = lax.rem(ctx + by, 8)
        copy = remote(leaving.at[to], landed.at[ctx], ctx_send.at[by - 1], ctx_recv.at[by - 1], (dp, to))
        copy.start()
        copies.append(copy)
    own.wait()
    for by in range(1, 8):
        source = lax.rem(ctx - by + 8, 8)
        remote(landed.at[source], landed.at[source], ctx_send.at[by - 1], ctx_recv.at[by - 1], (dp, source)).wait_recv()
    row = lax.broadcasted_iota(jnp.int32, (128, 128), 0)
    turn = (lax.broadcasted_iota(jnp.int32, (128, 128), 1) == (row % 8) * 16 + row // 8).astype(F32).astype(BF)
    turned[...] = jnp.dot(turn, landed[...].reshape(128, 1024), preferred_element_type=F32).reshape(16, 8, 1024).astype(BF)
    for by in range(1, 16):
        to = lax.rem(dp + by, 16)
        copy = remote(turned.at[to], arrived.at[dp], dp_send.at[by - 1], dp_recv.at[by - 1], (to, ctx))
        copy.start()
        copies.append(copy)
    own = pltpu.make_async_copy(turned.at[dp], arrived.at[dp], load.at[1])
    own.start()
    own.wait()
    for by in range(1, 16):
        source = lax.rem(dp - by + 16, 16)
        remote(arrived.at[source], arrived.at[source], dp_send.at[by - 1], dp_recv.at[by - 1], (source, ctx)).wait_recv()
    target = jnp.broadcast_to(upright(dest[...].reshape(1, 32) // 128), (32, 128))
    picking = (target == lax.broadcasted_iota(jnp.int32, (32, 128), 1).astype(F32)).astype(F32).astype(BF)
    came = arrived[...].astype(F32).reshape(128, 1024).astype(BF)
    visual_grad[...] = jnp.dot(picking, came, preferred_element_type=F32).astype(BF)
    for copy in copies:
        copy.wait_send()
    for chunk in ORDER:
        swaps[chunk].wait_send()
    ring_sum.finish()


def return_call(grads, placing, dest):
    shape = jax.ShapeDtypeStruct
    dma = pltpu.SemaphoreType.DMA
    return pl.pallas_call(
        return_kernel,
        out_shape=(shape((128, 1024), BF), shape((32, 1024), BF)),
        in_specs=[ANY, ANY, VM],
        out_specs=(VM, VM),
        scratch_shapes=[
            pltpu.VMEM((4, 128, 1024), BF), pltpu.VMEM((128, 128), BF),
            pltpu.VMEM((4, 128, 1024), BF), pltpu.VMEM((4, 128, 1024), BF),
            pltpu.VMEM((4, 128, 256), BF), pltpu.VMEM((4, 128, 256), BF), pltpu.VMEM((4, 128, 256), BF),
            pltpu.VMEM((8, 16, 1024), BF), pltpu.VMEM((8, 16, 1024), BF), pltpu.VMEM((16, 8, 1024), BF), pltpu.VMEM((16, 8, 1024), BF),
            dma((4,)), dma((4,)), dma((4,)), dma((12,)), dma((12,)), dma((15,)), dma((15,)), dma((7,)), dma((7,)),
        ],
        compiler_params=pltpu.CompilerParams(collective_id=3, has_side_effects=True, vmem_limit_bytes=VMEM_ALL),
        name="return_grads",
    )(grads, placing, dest)


def final_kernel(
    own_grad, visual_pair_grad, text_pairs, visual_pairs, weight, text, visual, gain, scales, marked, hidden_grad, visual_grad, means
):
    @pl.when(pl.program_id(0) == 0)
    def _():
        for rows, grad, pair in ((pl.ds(0, 128), own_grad, text_pairs), (pl.ds(128, 32), visual_pair_grad, visual_pairs)):
            mean = jnp.sum(grad[...].astype(F32) * pair[...].astype(F32), axis=-1, keepdims=True) * (1.0 / 8192.0)
            means[rows, :] = jnp.broadcast_to(mean, (rows.size, 128))

    block = weight[...]
    gains = gain[...]

    def through(grad, mean, value, scale):
        normed_grad = jnp.dot(grad, block, preferred_element_type=F32)
        return scale * (gains * normed_grad) - value.astype(F32) * (scale * scale * mean)

    full = through(own_grad[...], means[0:128, 0:1], text[...], scales[0:128, 0:1])
    hidden_grad[...] = jnp.where(marked[:, 0:1] > 0.5, 0.0, full).astype(BF)
    visual_grad[...] = through(visual_pair_grad[...], means[128:160, 0:1], visual[...], scales[128:160, 0:1]).astype(BF)


def final_call(own_grad, visual_pair_grad, text_pairs, visual_pairs, weight, text, visual, gain, scales, marked):
    shape = jax.ShapeDtypeStruct
    tile = 2048

    def whole(*dims):
        return pl.BlockSpec(dims, lambda i: (0,) * len(dims))

    return pl.pallas_call(
        final_kernel,
        out_shape=(shape((128, 8192), BF), shape((32, 8192), BF)),
        grid=(8192 // tile,),
        in_specs=[
            whole(128, 1024), whole(32, 1024), whole(128, 1024), whole(32, 1024),
            pl.BlockSpec((1024, tile), lambda i: (0, i)), pl.BlockSpec((128, tile), lambda i: (0, i)),
            pl.BlockSpec((32, tile), lambda i: (0, i)), pl.BlockSpec((1, tile), lambda i: (0, i)),
            whole(160, 128), whole(128, 128),
        ],
        out_specs=(pl.BlockSpec((128, tile), lambda i: (0, i)), pl.BlockSpec((32, tile), lambda i: (0, i))),
        scratch_shapes=[pltpu.VMEM((160, 128), F32)],
        compiler_params=pltpu.CompilerParams(vmem_limit_bytes=VMEM_ALL),
        name="through_norm",
    )(own_grad, visual_pair_grad, text_pairs, visual_pairs, weight, text, visual, gain, scales, marked)


def local(patches, vit_gain, merge_up, merge_down, dest, text, norm_gain, kv_weight, queries, out_grad, assign, docs):
    gain = norm_gain.reshape(1, 8192)
    text_all, visual_all, placing, marked, weight_t, text_pairs, visual_pairs, visual, scales = first_call(
        patches, vit_gain, merge_up, merge_down, text[0], gain, kv_weight, dest
    )
    own = lax.axis_index("ctx").astype(jnp.int32).reshape(1)
    attention, query_grad, pair_grads = attend_call(
        assign, own, text_all.reshape(8, 128, 1024), visual_all.reshape(8, 32, 1152), docs, queries[0], out_grad[0]
    )
    own_grad, visual_pair_grad = return_call(pair_grads.reshape(4, 2, 128, 1024), placing, dest)
    hidden_grad, visual_grad = final_call(
        own_grad, visual_pair_grad, text_pairs, visual_pairs, weight_t, text[0], visual, gain, scales, marked
    )
    return attention[None], query_grad[None], hidden_grad[None], visual_grad


def solution(mesh):
    placed = (
        P("dp", None),
        P(),
        P(None, "ctx"),
        P("ctx", None),
        P(("dp", "ctx")),
        P("dp", "ctx", None),
        P(),
        P(("dp", "ctx"), None),
        P("dp", "ctx", None),
        P("dp", "ctx", None),
        P(),
        P("dp", None),
    )
    return jax.shard_map(
        local,
        mesh=mesh,
        in_specs=placed,
        out_specs=(P("dp", "ctx", None), P("dp", "ctx", None), P("dp", "ctx", None), P(("dp", "ctx"), None)),
        check_vma=False,
    )
```
